128 devices in a mesh: gen: 4 (over z), learn: 32 (over x, y, core).
Axes of the slice: x: 4, y: 4, z: 4, core: 2. Of those that a mesh axis runs over, the one named last changes fastest.
Arguments:
- hidden: bfloat16 [32768, 5120], P(('gen', 'learn')), may hold values from -0.59765625 to 0.59765625
- cotangent: bfloat16 [32768, 1024], P(('gen', 'learn')), may hold values from -0.29882812 to 0.29882812
- importance: float32 [32768], P(('gen', 'learn')), may hold values from 0.25 to 4
- block_len: int32 [4096], P(('gen', 'learn')), may hold values from 1 to 8
- version: int32 [4096], P(('gen', 'learn')), may hold values from 0 to 3
- destination: int32 [4096, 1], P(('gen', 'learn')), may hold values from 0 to 31; in each aligned block of 32 rows (0 to 31, 32 to 63, ...) at most 2 rows name the same one
- w_key: bfloat16 [5120, 1024], replicated, may hold values from -0.078125 to 0.078125
- in_gain: float32 [5120], replicated, may hold values from 0.5 to 1.5
- key_gain: float32 [128], replicated, may hold values from 0.5 to 1.5
Outputs:
- grad_slots: bfloat16 [65536, 5120], P(('gen', 'learn'))
- w_grad: float32 [5120, 1024], P('gen')
- gain_grad: float32 [5120], replicated
- kgain_grad: float32 [128], replicated
The draws below stay inside these ranges and needn't reach their ends.
Inputs may be any that keep to these rules, and one draw needn't show every extreme that they name: `destination`: the 32 blocks of one device name each learner at most 2 times.
All inputs are finite; a program needn't handle non-finite values.
Results may differ from the reference program's by a relative error of at most 0.0075.
Values may be sent and summed in bfloat16 or wider, within the bound.
A program may use at most 128 MiB of HBM per device.

```python
import math
import jax
import jax.numpy as jnp
import numpy as np
from jax import lax

D = 5120
HD = 128
TILE = 8
VERSIONS = 4
SLOTS = 64
TPS = 32
KD = 1024
CAP = 2
NT = 4096
N_GEN = 4
N_LEARN = 32


def touch_ends(result, stream_key, low, largest):
    shape = result.shape
    place = [jax.random.randint(jax.random.fold_in(stream_key, axis), (), 0, shape[axis]) for axis in range(len(shape))]
    result = result.at[tuple(place)].set(low)
    longest = shape.index(max(shape))
    place[longest] = (place[longest] + 1) % shape[longest]
    return result.at[tuple(place)].set(largest)


def steps_of(stream_key, dims, cuts, smallest, top_value):
    factor_of = 1.0
    for dim, shards_of in cuts:
        heights = jax.random.uniform(jax.random.fold_in(jax.random.fold_in(stream_key, 6), dim), (shards_of,), jnp.float32, smallest / len(cuts), top_value / len(cuts))
        factor_of = factor_of * jnp.repeat(jnp.exp(heights), dims[dim] // shards_of).reshape((-1,) + (1,) * (len(dims) - 1 - dim))
    return factor_of


def routed_block(rng, own, number, rows, amount, top, bound, skew):
    sequence = jax.random.permutation(rng, amount)
    crowded, common = portions_of(amount, rows * top, bound, skew, True), portions_of(amount, rows * top, bound, skew, False)
    places = jnp.arange(amount)

    def named(sizes, turn):
        used = int((sizes > 0).sum())
        fixed = max(1, used // 4)
        passed = fixed + (places - fixed + turn * (used - fixed)) % max(1, amount - fixed)
        return jnp.zeros((amount,), jnp.int32).at[sequence[jnp.where(places < fixed, places, passed)]].set(jnp.asarray(sizes, jnp.int32))

    sizes = jnp.where(number % 4 == 0, named(crowded, number // 4), named(common, number - number // 4 - 1))
    mixed = jax.random.permutation(jax.random.fold_in(own, 3), amount)
    source_of, receiver = mixed[0:amount // 2 * 2:2], mixed[1:amount // 2 * 2:2]
    slack = jnp.minimum(sizes[source_of] - 1, bound - sizes[receiver]) // 2
    slack = jnp.where((source_of == sequence[0]) | (receiver == sequence[0]) | (sizes[receiver] == 0), 0, jnp.maximum(slack, 0))
    passed = jax.random.randint(jax.random.fold_in(own, 4), (amount // 2,), 0, 1 << 20) % (slack + 1)
    sizes = sizes.at[source_of].add(-passed).at[receiver].add(passed)
    labels = jnp.searchsorted(jnp.cumsum(sizes), jnp.arange(rows * top), side="right").astype(jnp.int32)
    table = labels.reshape(top, rows).T
    table = table[jax.random.permutation(jax.random.fold_in(own, 1), rows)]
    turn = jax.random.randint(jax.random.fold_in(own, 2), (rows, 1), 0, top)
    return jnp.take_along_axis(table, (jnp.arange(top)[None, :] + turn) % top, axis=1)


def portions_of(amount, total, limit, slope, full):
    portions = [(1 << 20) // math.isqrt(rank ** slope) + 1 for rank in range(1, amount + 1)]
    largest = limit if full else min(limit, max(-(-total // amount), total * portions[0] // sum(portions)))
    least = 1 if total - largest >= amount - 1 else 0
    holding, spare = [largest] + [least] * (amount - 1), total - largest - least * (amount - 1)
    while spare > 0:
        free = [i for i in range(1, amount) if holding[i] < largest] or [i for i in range(1, amount) if holding[i] < limit]
        whole, budget = sum([portions[i] for i in free]), spare
        for i in free:
            addition = min(limit - holding[i], max(1, budget * portions[i] // whole), spare)
            holding[i] = holding[i] + addition
            spare = spare - addition
    return np.array(holding)


def noise(rng, dims, width, reach, shards=(), kind=jnp.bfloat16):
    factor_of = steps_of(rng, dims, shards, -0.22, 0.18) if shards else 1.0
    drawn = jax.random.normal(rng, dims, jnp.float32) * width * factor_of
    return jnp.minimum(jnp.maximum(drawn, -reach), reach).astype(kind)


def setup_inputs(seed: int = 0) -> dict:
    key_of = jax.random.split(jax.random.key(seed), 10)
    hidden = noise(key_of[0], (NT * TILE, D), 0.1, 0.59765625, ((0, 128),))
    cotangent = noise(key_of[1], (NT * TILE, KD), 0.05, 0.29882812, ((0, 128),))
    importance = jnp.clip(jnp.exp(math.log(4.0) - 2.7725887 * jax.random.uniform(key_of[2], (NT * TILE,), jnp.float32) ** steps_of(key_of[2], (NT * TILE,), ((0, 128),), -0.2, 0.2)), 0.25, 4.0)
    block_len = touch_ends(jax.random.randint(key_of[3], (NT,), 1, TILE + 1), jax.random.fold_in(key_of[3], 1), 1, TILE).astype(jnp.int32)
    version = touch_ends(jax.random.randint(key_of[4], (NT,), 0, VERSIONS), jax.random.fold_in(key_of[4], 1), 0, VERSIONS - 1).astype(jnp.int32)
    destination_keys = jax.random.split(jax.random.fold_in(key_of[5], 1), NT // TPS)
    destination_turns = jax.random.permutation(jax.random.fold_in(key_of[5], 3), NT // TPS)
    destination = jax.vmap(lambda own, number: routed_block(jax.random.fold_in(key_of[5], 2), own, number, TPS, N_LEARN, 1, CAP, 2))(destination_keys, destination_turns).reshape((NT, 1))
    w_key = noise(key_of[6], (D, KD), D ** -0.5, 0.078125)
    in_gain = jnp.clip(1.0 + 0.1 * jax.random.normal(key_of[7], (D,), jnp.float32), 0.5, 1.5)
    key_gain = jnp.clip(1.0 + 0.1 * jax.random.normal(key_of[8], (HD,), jnp.float32), 0.5, 1.5)
    return {"hidden": hidden, "cotangent": cotangent, "importance": importance, "block_len": block_len, "version": version, "destination": destination, "w_key": w_key, "in_gain": in_gain, "key_gain": key_gain}


epsilon = 1e-06
clip_ratio = 2.0
staleness = 0.5

def token_weights(importance, block_len, version):
    tile_count = block_len.shape[0]
    inside = (lax.broadcasted_iota(jnp.int32, (tile_count, TILE), 1) < block_len[:, None]).astype(jnp.float32)
    stale_age = (VERSIONS - 1 - version).astype(jnp.float32)
    decay_factor = jnp.power(jnp.float32(staleness), stale_age)
    return jnp.minimum(importance, clip_ratio) * (decay_factor[:, None] * inside).reshape(-1)

def layer_pass(hidden, upstream_rows, w_key, in_gain, key_gain):
    row_count = hidden.shape[0]
    x_float = hidden.astype(jnp.float32)
    inv_rms = lax.rsqrt(lax.optimization_barrier(jnp.mean(x_float * x_float, -1, keepdims=True)) + epsilon)
    normed = x_float * inv_rms
    h_rows = (normed * in_gain).astype(jnp.bfloat16)
    key_rows = jnp.dot(h_rows, w_key, preferred_element_type=jnp.float32).reshape(row_count, -1, key_gain.shape[0])
    key_scale = lax.rsqrt(lax.optimization_barrier(jnp.mean(key_rows * key_rows, -1, keepdims=True)) + epsilon)
    upstream = upstream_rows.astype(jnp.float32).reshape(key_rows.shape)
    kgain_part = lax.optimization_barrier(jnp.sum(upstream * key_rows * key_scale, axis=(0, 1)))
    scaled = upstream * key_gain
    grad_keys = key_scale * scaled - key_rows * key_scale ** 3 * lax.optimization_barrier(jnp.mean(scaled * key_rows, -1, keepdims=True))
    grad_keys = grad_keys.reshape(row_count, -1).astype(jnp.bfloat16)
    grad_h = lax.dot_general(grad_keys, w_key, (((1,), (1,)), ((), ())), preferred_element_type=jnp.float32)
    gain_part = lax.optimization_barrier(jnp.sum(grad_h * normed, 0))
    grad_normed = grad_h * in_gain
    grad_input = inv_rms * (grad_normed - normed * lax.optimization_barrier(jnp.mean(grad_normed * normed, -1, keepdims=True)))
    return (grad_input.astype(jnp.bfloat16), h_rows, grad_keys, gain_part, kgain_part)

def reference(hidden, cotangent, importance, block_len, version, destination, w_key, in_gain, key_gain):
    weights = token_weights(importance, block_len, version)
    upstream_all = (cotangent.astype(jnp.float32) * weights[:, None]).astype(jnp.bfloat16)
    device_count = N_GEN * N_LEARN
    per_device = TPS * TILE

    def scan_step(totals, block_pair):
        hidden_block, upstream_block = block_pair
        grad_input, h_rows, grad_keys, gain_part, kgain_part = layer_pass(hidden_block, upstream_block, w_key, in_gain, key_gain)
        weight_sum = totals[0] + lax.dot_general(h_rows, grad_keys, (((0,), (0,)), ((), ())), preferred_element_type=jnp.float32)
        return ((weight_sum, totals[1] + gain_part, totals[2] + kgain_part), grad_input)
    initial = (jnp.zeros((D, KD), jnp.float32), jnp.zeros((D,), jnp.float32), jnp.zeros((HD,), jnp.float32))
    totals, grad_blocks = lax.scan(scan_step, initial, (hidden.reshape(device_count, per_device, D), upstream_all.reshape(device_count, per_device, KD)))
    grad_tiles = grad_blocks.reshape(device_count * TPS, TILE, D)
    dest_device = destination[:, 0].reshape(device_count, TPS)
    onehot = (dest_device[:, :, None] == jnp.arange(N_LEARN, dtype=jnp.int32)[None, None, :]).astype(jnp.int32)
    slot_rank = lax.optimization_barrier(jnp.sum((jnp.cumsum(onehot, 1) - onehot) * onehot, -1))
    device_ids = jnp.arange(device_count, dtype=jnp.int32)[:, None]
    gen_ids = device_ids // N_LEARN
    learn_ids = device_ids % N_LEARN
    target = ((gen_ids * N_LEARN + dest_device) * SLOTS + learn_ids * CAP + slot_rank).reshape(-1)
    slots_out = jnp.zeros((device_count * SLOTS, TILE, D), jnp.bfloat16).at[target].set(grad_tiles)
    return (slots_out.reshape(-1, D), totals[0], totals[1], totals[2])
```

```python
import functools

import jax
import jax.numpy as jnp
from jax import lax
from jax.experimental import pallas as pl
from jax.experimental.pallas import tpu as pltpu
from jax.sharding import PartitionSpec as P

MESH = pl.DeviceIdType.MESH
F32 = jnp.float32
BF16 = jnp.bfloat16

D = 5120
KD = 1024
HD = 128
ROWS = 256
TILE = 8
SR = 512
PAIR = 16
PIECE = D // 8
EPS = 1e-06

OTHERS = (
    (1, 0), (3, 0), (0, 1), (0, 3), (1, 1), (3, 3), (1, 3), (3, 1),
    (2, 0), (0, 2), (2, 1), (1, 2), (2, 3), (3, 2), (2, 2),
)
ORDER = ((0, 0, 1),) + tuple((a, b, c) for (a, b) in OTHERS for c in range(2))
ZPEERS = ((0, 1), (1, 0), (3, 0), (1, 1), (3, 1), (2, 0), (2, 1))


def ds(start, size, mult=None):
    return pl.ds(start if mult is None else pl.multiple_of(start, mult), size)


def kernel(
    hid, cot, imp, blen, ver, dest, w, gain, kgain,
    slots_out, w_out, g_out,
    x_v, w_v, cot_v, inv_v, cw_v, h_v, gk_v, msum_v, place_v, slots_v, hbuf, gkbuf, acc,
    rs1s, rs1r, rs2s, rs2r, wbuf, gbuf1, gbuf2, gbuf3,
    in_sem, w_sem, own_sem, h_ss, h_rs, k_ss, k_rs, rel_ss, s_ss, s_rs,
    r1_ss, r1_rs, r2_ss, r2_rs, ab_ss, ab_rs, aa_ss, aa_rs, ac_ss, ac_rs,
    g1_ss, g1_rs, g2_ss, g2_rs, g3_ss, g3_rs,
):
    g = lax.axis_index("gen")
    l = lax.axis_index("learn")
    x = l // 8
    y = (l // 2) % 4
    c = l % 2
    a = x + c * (y - x)
    b = y + c * (x - y)
    me = g * 2 + c

    def plane(px, py, pc):
        return (g, px * 8 + py * 2 + pc)

    def a_dev(na):
        return plane(x + (1 - c) * (na - x), y + c * (na - y), c)

    def b_dev(nb):
        return plane(x + c * (nb - x), y + (1 - c) * (nb - y), c)

    def z_dev(q, pc):
        return (q, x * 8 + y * 2 + pc)

    def remote(src, dst, ss, rs, dev):
        return pltpu.make_async_remote_copy(src, dst, ss, rs, device_id=dev, device_id_type=MESH)

    for i in range(4):
        rows = ds(i * 64, 64)
        pltpu.make_async_copy(hid.at[rows], x_v.at[rows], in_sem.at[i]).start()
    pltpu.make_async_copy(cot, cot_v, in_sem.at[4]).start()
    for n in range(4):
        cols = ds(n * 256, 256)
        pltpu.make_async_copy(w.at[:, cols], w_v.at[:, cols], w_sem.at[n]).start()

    barrier = pltpu.get_barrier_semaphore()

    @pl.loop(1, 32)
    def _(i):
        pl.semaphore_signal(barrier, inc=1, device_id=(g, lax.rem(l + i, 32)), device_id_type=MESH)

    for dz, dc in ZPEERS[1:]:
        pl.semaphore_signal(
            barrier, inc=1, device_id=z_dev(lax.rem(g + dz, 4), lax.rem(c + dc, 2)), device_id_type=MESH
        )

    r256 = lax.broadcasted_iota(jnp.int32, (ROWS, ROWS), 0)
    j256 = lax.broadcasted_iota(jnp.int32, (ROWS, ROWS), 1)
    imp_col = jnp.sum(jnp.where(r256 == j256, imp[...], 0.0), axis=1, keepdims=True)
    r32 = lax.broadcasted_iota(jnp.int32, (ROWS, 32), 0)
    j32 = lax.broadcasted_iota(jnp.int32, (ROWS, 32), 1)
    of_block = (r32 >> 3) == j32
    len_col = jnp.sum(jnp.where(of_block, blen[...].astype(F32), 0.0), axis=1, keepdims=True)
    ver_col = jnp.sum(jnp.where(of_block, ver[...].astype(F32), 0.0), axis=1, keepdims=True)
    row_col = (lax.broadcasted_iota(jnp.int32, (ROWS, 1), 0) & 7).astype(F32)
    inside = jnp.where(row_col < len_col, 1.0, 0.0)
    age = 3.0 - ver_col
    decay = jnp.where(age == 0.0, 1.0, jnp.where(age == 1.0, 0.5, jnp.where(age == 2.0, 0.25, 0.125)))
    cw_v[...] = jnp.broadcast_to(jnp.minimum(imp_col, 2.0) * (decay * inside), (ROWS, HD))

    blk = lax.broadcasted_iota(jnp.int32, (32, ROWS), 0)
    row_blk = lax.broadcasted_iota(jnp.int32, (32, ROWS), 1) >> 3
    dest_col = dest[...].astype(F32)
    dest_row = jnp.sum(jnp.where(blk == row_blk, dest_col, 0.0), axis=0, keepdims=True)
    rank_row = jnp.sum(jnp.where((blk < row_blk) & (dest_col == dest_row), 1.0, 0.0), axis=0, keepdims=True)
    target = dest_row * 2.0 + rank_row
    srow = lax.broadcasted_iota(jnp.int32, (SR, ROWS), 0)
    scol = lax.broadcasted_iota(jnp.int32, (SR, ROWS), 1)
    hit = ((srow >> 3).astype(F32) == target) & ((srow & 7) == (scol & 7))
    place_v[...] = jnp.where(hit, 1.0, 0.0).astype(BF16)

    @pl.loop(0, 4)
    def _(i):
        big = ds(i * 64, 64, 64)
        pltpu.make_async_copy(hid.at[big], x_v.at[big], in_sem.at[i]).wait()

        @pl.loop(0, 4)
        def _(k):
            rows = ds(i * 64 + k * 16, 16, 16)
            total = jnp.zeros((16, HD), F32)
            for f in range(D // HD):
                xf = x_v[rows, f * HD : (f + 1) * HD].astype(F32)
                total = total + xf * xf
            inv = lax.rsqrt(jnp.sum(total, axis=1, keepdims=True) * (1.0 / D) + EPS)
            inv = jnp.broadcast_to(inv, (16, HD))
            inv_v[rows, :] = inv
            for f in range(D // HD):
                cols = slice(f * HD, (f + 1) * HD)
                h_v[rows, cols] = (x_v[rows, cols].astype(F32) * inv * gain[:, cols]).astype(BF16)

    pl.semaphore_wait(barrier, 31 + 6)

    h_copies = []
    for i, (dz, dc) in enumerate(ZPEERS):
        q, pc = lax.rem(g + dz, 4), lax.rem(c + dc, 2)
        piece = h_v.at[:, ds((q * 2 + pc) * PIECE, PIECE, 128)]
        copy = remote(piece, hbuf.at[me], h_ss.at[i], h_rs.at[me], z_dev(q, pc))
        copy.start()
        h_copies.append(copy)

    pltpu.make_async_copy(cot, cot_v, in_sem.at[4]).wait()
    msum_v[...] = jnp.zeros((ROWS, HD), F32)

    def key_tile(n, kg):
        cols = ds(n * 256, 256, 256)
        pltpu.make_async_copy(w.at[:, cols], w_v.at[:, cols], w_sem.at[n]).wait()
        keys = jnp.dot(h_v[...], w_v[:, cols], preferred_element_type=F32)
        for s in range(2):
            k = keys[:, s * HD : (s + 1) * HD]
            head = ds(n * 256 + s * HD, HD, HD)
            scale = lax.rsqrt(jnp.sum(k * k, axis=1, keepdims=True) * (1.0 / HD) + EPS)
            up = (cot_v[:, head].astype(F32) * cw_v[...]).astype(BF16).astype(F32)
            kg = kg + jnp.sum(up * k * scale, axis=0, keepdims=True)
            u = up * kgain[...]
            mean = jnp.sum(u * k, axis=1, keepdims=True) * (1.0 / HD)
            gk = (scale * u - k * (scale * scale * scale) * mean).astype(BF16)
            gk_v[:, head] = gk
            msum_v[...] += gk.astype(F32) * k
        return kg

    kg = lax.fori_loop(0, 4, key_tile, jnp.zeros((1, HD), F32))
    gbuf1[me, :, D:] = kg

    k_copies = []
    for i, (dz, dc) in enumerate(((0, 1), (1, 0), (3, 0), (2, 0))):
        q, pc = lax.rem(g + dz, 4), lax.rem(c + dc, 2)
        copy = remote(gk_v, gkbuf.at[me], k_ss.at[i], k_rs.at[me], z_dev(q, pc))
        copy.start()
        k_copies.append(copy)

    mean = jnp.sum(msum_v[...], axis=1, keepdims=True) * (1.0 / D)
    msum_v[...] = jnp.broadcast_to(mean, (ROWS, HD))

    @pl.loop(0, 4)
    def _(q):
        @pl.loop(0, 5)
        def _(s):
            f = pl.multiple_of(q * 1280 + s * 256, 256)
            cols = pl.ds(f, 256)
            grad_h = lax.dot_general(
                gk_v[...], w_v[cols, :], (((1,), (1,)), ((), ())), preferred_element_type=F32
            )
            inv = jnp.concatenate([inv_v[...]] * 2, axis=1)
            mean = jnp.concatenate([msum_v[...]] * 2, axis=1)
            normed = x_v[:, cols].astype(F32) * inv
            gbuf1[me, :, cols] = jnp.sum(grad_h * normed, axis=0, keepdims=True)
            grad_in = (inv * (grad_h * gain[:, cols] - normed * mean)).astype(BF16)
            slots_v[:, cols] = jnp.dot(place_v[...], grad_in, preferred_element_type=F32).astype(BF16)

        quarter = ds(q * 1280, 1280, 1280)
        for dx, dy, dc in ORDER:
            dev = plane(lax.rem(x + dx, 4), lax.rem(y + dy, 4), lax.rem(c + dc, 2))
            remote(
                slots_v.at[ds(dev[1] * PAIR, PAIR, PAIR), quarter],
                slots_out.at[ds(l * PAIR, PAIR, PAIR), quarter],
                s_ss, s_rs, dev,
            ).start()

    mine = ds(l * PAIR, PAIR, PAIR)
    own = pltpu.make_async_copy(slots_v.at[mine], slots_out.at[mine], own_sem)
    own.start()

    def broadcast(buf, place, peers, ss, rs):
        copies = []
        for i, dev in enumerate(peers):
            copy = remote(buf.at[place], buf.at[place], ss.at[i], rs.at[place], dev)
            copy.start()
            copies.append(copy)
        return copies

    def arrived(buf, place, rs):
        remote(buf.at[place], buf.at[place], rs.at[place], rs.at[place], (g, l)).wait_recv()

    g_copies = broadcast(
        gbuf1, me, [z_dev(lax.rem(g + dz, 4), lax.rem(c + dc, 2)) for dz, dc in ZPEERS], g1_ss, g1_rs
    )

    def add(hs, gks, first=False):
        part = lax.dot_general(hs, gks, (((0,), (0,)), ((), ())), preferred_element_type=F32)
        if first:
            acc[...] = part
        else:
            acc[...] += part

    add(h_v[:, ds(me * PIECE, PIECE, 128)], gk_v[...], True)
    partner = z_dev(g, 1 - c)
    other = g * 2 + 1 - c
    arrived(hbuf, other, h_rs)
    arrived(gkbuf, other, k_rs)
    add(hbuf[other], gkbuf[other])

    for dz, dc in ZPEERS:
        arrived(gbuf1, lax.rem(g + dz, 4) * 2 + lax.rem(c + dc, 2), g1_rs)
    total = gbuf1[0]
    for i in range(1, 8):
        total = total + gbuf1[i]
    gbuf2[x] = total
    g_copies += broadcast(gbuf2, x, [plane(lax.rem(x + d, 4), y, c) for d in (1, 3, 2)], g2_ss, g2_rs)

    rel_copies = []
    for i, dz in enumerate((1, 3, 2)):
        q = lax.rem(g + dz, 4)
        same, cross = q * 2 + c, q * 2 + 1 - c
        arrived(gkbuf, same, k_rs)
        copy = remote(gkbuf.at[same], gkbuf.at[same], rel_ss.at[i], k_rs.at[same], partner)
        copy.start()
        rel_copies.append(copy)
        arrived(hbuf, same, h_rs)
        add(hbuf[same], gkbuf[same])
        arrived(hbuf, cross, h_rs)
        arrived(gkbuf, cross, k_rs)
        add(hbuf[cross], gkbuf[cross])

    rs1s[...] = acc[...].astype(BF16)
    w_copies = []
    for i, d in enumerate((1, 3, 2)):
        na = lax.rem(a + d, 4)
        copy = remote(rs1s.at[ds(na * 160, 160, 16)], rs1r.at[a], r1_ss.at[i], r1_rs.at[a], a_dev(na))
        copy.start()
        w_copies.append(copy)

    for d in (1, 3, 2):
        arrived(gbuf2, lax.rem(x + d, 4), g2_rs)
    gbuf3[y] = (gbuf2[0] + gbuf2[1]) + (gbuf2[2] + gbuf2[3])
    g_copies += broadcast(gbuf3, y, [plane(x, lax.rem(y + d, 4), c) for d in (1, 3, 2)], g3_ss, g3_rs)

    held = acc.at[ds(a * 160, 160, 8)]
    for d in (1, 3, 2):
        na = lax.rem(a + d, 4)
        arrived(rs1r, na, r1_rs)
        held[...] += rs1r[na].astype(F32)
    for n in range(4):
        rs2s[n] = held[:, n * 256 : (n + 1) * 256].astype(BF16)
    for i, d in enumerate((1, 3, 2)):
        nb = lax.rem(b + d, 4)
        copy = remote(rs2s.at[nb], rs2r.at[b], r2_ss.at[i], r2_rs.at[b], b_dev(nb))
        copy.start()
        w_copies.append(copy)
    total = held[:, ds(b * 256, 256, 256)]
    for d in (1, 3, 2):
        nb = lax.rem(b + d, 4)
        arrived(rs2r, nb, r2_rs)
        total = total + rs2r[nb].astype(F32)

    def rows_of(na, pc):
        return ds(pc * 640 + na * 160, 160, 16)

    def block(na, nb):
        return wbuf.at[rows_of(na, c), ds(nb * 256, 256, 256)]

    wbuf[rows_of(a, c), ds(b * 256, 256, 256)] = total.astype(BF16)
    for i, d in enumerate((1, 3, 2)):
        copy = remote(block(a, b), block(a, b), ab_ss.at[i], ab_rs.at[b], b_dev(lax.rem(b + d, 4)))
        copy.start()
        w_copies.append(copy)
    for d in (1, 3, 2):
        nb = lax.rem(b + d, 4)
        remote(block(a, nb), block(a, nb), ab_rs.at[nb], ab_rs.at[nb], (g, l)).wait_recv()
    band = wbuf.at[rows_of(a, c)]
    for i, d in enumerate((1, 3, 2)):
        copy = remote(band, band, aa_ss.at[i], aa_rs.at[a], a_dev(lax.rem(a + d, 4)))
        copy.start()
        w_copies.append(copy)
    copy = remote(band, band, ac_ss.at[0], ac_rs.at[a], partner)
    copy.start()
    w_copies.append(copy)
    for i, d in enumerate((1, 3, 2)):
        na = lax.rem(a + d, 4)
        band = wbuf.at[rows_of(na, c)]
        remote(band, band, aa_rs.at[na], aa_rs.at[na], (g, l)).wait_recv()
        copy = remote(band, band, ac_ss.at[i + 1], ac_rs.at[na], partner)
        copy.start()
        w_copies.append(copy)
    for n in range(4):
        band = wbuf.at[rows_of(n, 1 - c)]
        remote(band, band, ac_rs.at[n], ac_rs.at[n], (g, l)).wait_recv()
    out = pltpu.make_async_copy(wbuf, w_out, in_sem.at[0])
    out.start()

    for d in (1, 3, 2):
        arrived(gbuf3, lax.rem(y + d, 4), g3_rs)
    g_out[...] = (gbuf3[0] + gbuf3[1]) + (gbuf3[2] + gbuf3[3])

    for copy in h_copies + k_copies + g_copies + rel_copies + w_copies:
        copy.wait_send()
    own.wait()
    everyone = remote(slots_v.at[ds(0, 31 * PAIR)], slots_out.at[ds(0, 31 * PAIR)], s_ss, s_rs, (g, l))
    everyone.wait_send()
    everyone.wait_recv()
    out.wait()


def body(hidden, cotangent, importance, block_len, version, destination, w_key, in_gain, key_gain):
    dma = pltpu.SemaphoreType.DMA
    vmem = pl.BlockSpec(memory_space=pltpu.VMEM)
    hbm = pl.BlockSpec(memory_space=pl.ANY)
    slots, w_rows, gains = pl.pallas_call(
        kernel,
        name="grad_step",
        out_shape=(
            jax.ShapeDtypeStruct((SR, D), BF16),
            jax.ShapeDtypeStruct((D // 4, KD), BF16),
            jax.ShapeDtypeStruct((1, D + HD), F32),
        ),
        in_specs=[hbm, hbm, vmem, vmem, vmem, vmem, hbm, vmem, vmem],
        out_specs=(hbm, hbm, vmem),
        scratch_shapes=[
            pltpu.VMEM((ROWS, D), BF16),
            pltpu.VMEM((D, KD), BF16),
            pltpu.VMEM((ROWS, KD), BF16),
            pltpu.VMEM((ROWS, HD), F32),
            pltpu.VMEM((ROWS, HD), F32),
            pltpu.VMEM((ROWS, D), BF16),
            pltpu.VMEM((ROWS, KD), BF16),
            pltpu.VMEM((ROWS, HD), F32),
            pltpu.VMEM((SR, ROWS), BF16),
            pltpu.VMEM((SR, D), BF16),
            pltpu.VMEM((8, ROWS, PIECE), BF16),
            pltpu.VMEM((8, ROWS, KD), BF16),
            pltpu.VMEM((PIECE, KD), F32),
            pltpu.VMEM((PIECE, KD), BF16),
            pltpu.VMEM((4, 160, KD), BF16),
            pltpu.VMEM((4, 160, 256), BF16),
            pltpu.VMEM((4, 160, 256), BF16),
            pltpu.VMEM((D // 4, KD), BF16),
            pltpu.VMEM((8, 1, D + HD), F32),
            pltpu.VMEM((4, 1, D + HD), F32),
            pltpu.VMEM((4, 1, D + HD), F32),
            dma((5,)), dma((4,)), dma(()),
            dma((7,)), dma((8,)), dma((4,)), dma((8,)), dma((3,)), dma(()), dma(()),
            dma((3,)), dma((4,)), dma((3,)), dma((4,)),
            dma((3,)), dma((4,)), dma((3,)), dma((4,)), dma((4,)), dma((4,)),
            dma((7,)), dma((8,)), dma((3,)), dma((4,)), dma((3,)), dma((4,)),
        ],
        compiler_params=pltpu.CompilerParams(
            collective_id=0, has_side_effects=True, vmem_limit_bytes=60 * 1024 * 1024
        ),
    )(
        hidden, cotangent, importance.reshape(1, ROWS), block_len.reshape(1, 32),
        version.reshape(1, 32), destination, w_key, in_gain.reshape(1, D), key_gain.reshape(1, HD),
    )
    return slots, w_rows.astype(F32), gains[0, :D], gains[0, D:]


def solution(mesh):
    return jax.shard_map(
        body,
        mesh=mesh,
        in_specs=(
            P(("gen", "learn"), None),
            P(("gen", "learn"), None),
            P(("gen", "learn")),
            P(("gen", "learn")),
            P(("gen", "learn")),
            P(("gen", "learn"), None),
            P(),
            P(),
            P(),
        ),
        out_specs=(P(("gen", "learn"), None), P("gen", None), P(), P()),
        check_vma=False,
    )
```

```python
import functools

import jax
import jax.numpy as jnp
from jax import lax
from jax.experimental import pallas as pl
from jax.experimental.pallas import tpu as pltpu
from jax.sharding import PartitionSpec as P

MESH = pl.DeviceIdType.MESH
F32 = jnp.float32
BF16 = jnp.bfloat16

D = 5120
KD = 1024
HD = 128
ROWS = 256
TILE = 8
SR = 512
PAIR = 16
PIECE = D // 8
FC = 128
NC = PIECE // FC
TW = 256
EPS = 1e-06

OTHERS = (
    (1, 0), (3, 0), (0, 1), (0, 3), (1, 1), (3, 3), (1, 3), (3, 1),
    (2, 0), (0, 2), (2, 1), (1, 2), (2, 3), (3, 2), (2, 2),
)
ORDER = ((0, 0, 1),) + tuple((a, b, c) for (a, b) in OTHERS for c in range(2))
ZPEERS = ((0, 1), (1, 0), (3, 0), (1, 1), (3, 1), (2, 0), (2, 1))


def ds(start, size, mult=None):
    return pl.ds(start if mult is None else pl.multiple_of(start, mult), size)


def kernel(
    hid, cot, imp, blen, ver, dest, w, gain, kgain,
    slots_out, w_out, g_out, kg_out,
    x_v, w_v, cot_v, inv_v, cw_v, h_v, msum_v, place_v, slots_v, hbuf, gkbuf, acc, tot_v,
    rs1s, rs1r, rs2s, rs2r, wbuf, gbuf1, gbuf2, gbuf3,
    in_sem, w_sem, own_sem, h_ss, h_rs, k_ss, k_rs, rel_ss, s_ss, s_rs,
    r1_ss, r1_rs, r2_ss, r2_rs, ab_ss, ab_rs, aa_ss, aa_rs, ac_ss, ac_rs,
    g1_ss, g1_rs, g2_ss, g2_rs, g3_ss, g3_rs,
):
    g = lax.axis_index("gen")
    l = lax.axis_index("learn")
    x = l // 8
    y = (l // 2) % 4
    c = l % 2
    a = x + c * (y - x)
    b = y + c * (x - y)
    me = g * 2 + c

    def plane(px, py, pc):
        return (g, px * 8 + py * 2 + pc)

    def a_dev(na):
        return plane(x + (1 - c) * (na - x), y + c * (na - y), c)

    def b_dev(nb):
        return plane(x + c * (nb - x), y + (1 - c) * (nb - y), c)

    def z_dev(q, pc):
        return (q, x * 8 + y * 2 + pc)

    def remote(src, dst, ss, rs, dev):
        return pltpu.make_async_remote_copy(src, dst, ss, rs, device_id=dev, device_id_type=MESH)

    for i in range(4):
        rows = ds(i * 64, 64)
        pltpu.make_async_copy(hid.at[rows], x_v.at[rows], in_sem.at[i]).start()
    for n in range(4):
        cols = ds(n * 256, 256)
        pltpu.make_async_copy(w.at[:, cols], w_v.at[:, cols], w_sem.at[n]).start()
    pltpu.make_async_copy(cot, cot_v, in_sem.at[4]).start()

    barrier = pltpu.get_barrier_semaphore()

    @pl.loop(1, 32)
    def _(i):
        pl.semaphore_signal(barrier, inc=1, device_id=(g, lax.rem(l + i, 32)), device_id_type=MESH)

    for dz, dc in ZPEERS[1:]:
        pl.semaphore_signal(
            barrier, inc=1, device_id=z_dev(lax.rem(g + dz, 4), lax.rem(c + dc, 2)), device_id_type=MESH
        )

    r256 = lax.broadcasted_iota(jnp.int32, (ROWS, ROWS), 0)
    j256 = lax.broadcasted_iota(jnp.int32, (ROWS, ROWS), 1)
    imp_col = jnp.sum(jnp.where(r256 == j256, imp[...], 0.0), axis=1, keepdims=True)
    r32 = lax.broadcasted_iota(jnp.int32, (ROWS, 32), 0)
    j32 = lax.broadcasted_iota(jnp.int32, (ROWS, 32), 1)
    of_block = (r32 >> 3) == j32
    len_col = jnp.sum(jnp.where(of_block, blen[...].astype(F32), 0.0), axis=1, keepdims=True)
    ver_col = jnp.sum(jnp.where(of_block, ver[...].astype(F32), 0.0), axis=1, keepdims=True)
    row_col = (lax.broadcasted_iota(jnp.int32, (ROWS, 1), 0) & 7).astype(F32)
    inside = jnp.where(row_col < len_col, 1.0, 0.0)
    age = 3.0 - ver_col
    decay = jnp.where(age == 0.0, 1.0, jnp.where(age == 1.0, 0.5, jnp.where(age == 2.0, 0.25, 0.125)))
    cw_v[...] = jnp.broadcast_to(jnp.minimum(imp_col, 2.0) * (decay * inside), (ROWS, HD))

    b32 = lax.broadcasted_iota(jnp.int32, (32, 32), 0)
    e32 = lax.broadcasted_iota(jnp.int32, (32, 32), 1)
    dest_col = jnp.sum(jnp.where(b32 == e32, dest[...].astype(F32), 0.0), axis=1, keepdims=True)
    blk = lax.broadcasted_iota(jnp.int32, (32, ROWS), 0)
    row_blk = lax.broadcasted_iota(jnp.int32, (32, ROWS), 1) >> 3
    dest_row = jnp.sum(jnp.where(blk == row_blk, dest_col, 0.0), axis=0, keepdims=True)
    rank_row = jnp.sum(jnp.where((blk < row_blk) & (dest_col == dest_row), 1.0, 0.0), axis=0, keepdims=True)
    target = dest_row * 2.0 + rank_row
    srow = lax.broadcasted_iota(jnp.int32, (SR, ROWS), 0)
    scol = lax.broadcasted_iota(jnp.int32, (SR, ROWS), 1)
    hit = ((srow >> 3).astype(F32) == target) & ((srow & 7) == (scol & 7))
    place_v[...] = jnp.where(hit, 1.0, 0.0).astype(BF16)

    @pl.loop(0, 4)
    def _(i):
        big = ds(i * 64, 64, 64)
        pltpu.make_async_copy(hid.at[big], x_v.at[big], in_sem.at[i]).wait()
        invs = []
        for k in range(4):
            rows = ds(i * 64 + k * 16, 16, 16)
            total = jnp.zeros((16, HD), F32)
            for f in range(D // HD):
                xf = x_v[rows, f * HD : (f + 1) * HD].astype(F32)
                total = total + xf * xf
            inv = lax.rsqrt(jnp.sum(total, axis=1, keepdims=True) * (1.0 / D) + EPS)
            inv = jnp.broadcast_to(inv, (16, HD))
            inv_v[rows, :] = inv
            invs.append(inv)
        for k in range(4):
            rows = ds(i * 64 + k * 16, 16, 16)
            for f in range(D // HD):
                cols = slice(f * HD, (f + 1) * HD)
                h_v[rows, cols] = (x_v[rows, cols].astype(F32) * invs[k] * gain[:, cols]).astype(BF16)

    pl.semaphore_wait(barrier, 31 + 6)

    def mine(ref):
        return ref.at[ds(me * ROWS, ROWS, ROWS)]

    def send_h(k):
        for dz, dc in ZPEERS:
            q, pc = lax.rem(g + dz, 4), lax.rem(c + dc, 2)
            piece = h_v.at[:, ds((q * 2 + pc) * PIECE + k * FC, FC, FC)]
            remote(piece, mine(hbuf.at[k]), h_ss, h_rs.at[k, me], z_dev(q, pc)).start()

    send_h(0)
    for k in range(NC):
        hbuf[k, ds(me * ROWS, ROWS, ROWS), :] = h_v[:, ds(me * PIECE + k * FC, FC, FC)]

    pltpu.make_async_copy(cot, cot_v, in_sem.at[4]).wait()
    for n in range(4):
        cols = ds(n * 256, 256)
        pltpu.make_async_copy(w.at[:, cols], w_v.at[:, cols], w_sem.at[n]).wait()
    kg = jnp.zeros((1, HD), F32)
    for n in range(4):
        keys = jnp.dot(h_v[...], w_v[:, n * 256 : (n + 1) * 256], preferred_element_type=F32)
        for s in range(2):
            k = keys[:, s * HD : (s + 1) * HD]
            head = slice(n * 256 + s * HD, n * 256 + s * HD + HD)
            scale = lax.rsqrt(jnp.sum(k * k, axis=1, keepdims=True) * (1.0 / HD) + EPS)
            up = (cot_v[:, head].astype(F32) * cw_v[...]).astype(BF16).astype(F32)
            kg = kg + jnp.sum(up * k * scale, axis=0, keepdims=True)
            u = up * kgain[...]
            mean = jnp.sum(u * k, axis=1, keepdims=True) * (1.0 / HD)
            gk = (scale * u - k * (scale * scale * scale) * mean).astype(BF16)
            gkbuf[ds(me * ROWS, ROWS, ROWS), head] = gk
            if n + s == 0:
                msum_v[...] = gk.astype(F32) * k
            else:
                msum_v[...] += gk.astype(F32) * k
    gbuf1[me, :, D:] = kg

    for dz, dc in ((0, 1), (1, 0), (3, 0), (2, 0)):
        q, pc = lax.rem(g + dz, 4), lax.rem(c + dc, 2)
        remote(mine(gkbuf), mine(gkbuf), k_ss, k_rs.at[me], z_dev(q, pc)).start()
    for k in range(1, NC):
        send_h(k)

    mean = jnp.sum(msum_v[...], axis=1, keepdims=True) * (1.0 / D)
    msum_v[...] = jnp.broadcast_to(mean, (ROWS, HD))

    def send_slots(q, order):
        quarter = ds(q * 1280, 1280, 1280)
        for dx, dy, dc in order:
            dev = plane(lax.rem(x + dx, 4), lax.rem(y + dy, 4), lax.rem(c + dc, 2))
            remote(
                slots_v.at[ds(dev[1] * PAIR, PAIR, PAIR), quarter],
                slots_out.at[ds(l * PAIR, PAIR, PAIR), quarter],
                s_ss, s_rs, dev,
            ).start()

    def quarter_of(q):
        for s in range(1280 // TW):
            cols = pl.ds(pl.multiple_of(q * 1280 + s * TW, TW), TW)
            grad_h = lax.dot_general(
                mine(gkbuf)[...], w_v[cols, :], (((1,), (1,)), ((), ())), preferred_element_type=F32
            )
            inv = jnp.concatenate([inv_v[...]] * (TW // HD), axis=1)
            mean = jnp.concatenate([msum_v[...]] * (TW // HD), axis=1)
            normed = x_v[:, cols].astype(F32) * inv
            gbuf1[me, :, cols] = jnp.sum(grad_h * normed, axis=0, keepdims=True)
            grad_in = (inv * (grad_h * gain[:, cols] - normed * mean)).astype(BF16)
            slots_v[:, cols] = jnp.dot(place_v[...], grad_in, preferred_element_type=F32).astype(BF16)

    @pl.loop(0, 2)
    def _(q):
        quarter_of(q)
        send_slots(q, ORDER)

    @pl.loop(2, 4)
    def _(q):
        quarter_of(q)

    own_rows = ds(l * PAIR, PAIR, PAIR)
    own = pltpu.make_async_copy(slots_v.at[own_rows], slots_out.at[own_rows], own_sem)
    own.start()
    groups = (ORDER[:9], ORDER[9:17], ORDER[17:25], ORDER[25:])
    held_back = [(q, order) for q in (2, 3) for order in groups]

    def send_more(count):
        for _ in range(count):
            if held_back:
                send_slots(*held_back.pop(0))

    def broadcast(buf, place, peers, ss, rs):
        copies = []
        for i, dev in enumerate(peers):
            copy = remote(buf.at[place], buf.at[place], ss.at[i], rs.at[place], dev)
            copy.start()
            copies.append(copy)
        return copies

    def arrived(ref, rs):
        remote(ref, ref, rs, rs, (g, l)).wait_recv()

    g_copies = broadcast(
        gbuf1, me, [z_dev(lax.rem(g + dz, 4), lax.rem(c + dc, 2)) for dz, dc in ZPEERS], g1_ss, g1_rs
    )
    partner = z_dev(g, 1 - c)

    def of(ref, src):
        return ref.at[ds(src * ROWS, ROWS, ROWS)]

    for dz in (1, 3, 2):
        same = lax.rem(g + dz, 4) * 2 + c
        arrived(of(gkbuf, same), k_rs.at[same])
        remote(of(gkbuf, same), of(gkbuf, same), rel_ss, k_rs.at[same], partner).start()
    for dz in (0, 1, 3, 2):
        cross = lax.rem(g + dz, 4) * 2 + 1 - c
        arrived(of(gkbuf, cross), k_rs.at[cross])

    def stage0(k):
        for dz, dc in ZPEERS:
            src = lax.rem(g + dz, 4) * 2 + lax.rem(c + dc, 2)
            arrived(of(hbuf.at[k], src), h_rs.at[k, src])
        part = lax.dot_general(
            hbuf[k], gkbuf[...], (((0,), (0,)), ((), ())), preferred_element_type=F32
        )
        acc[k % 2] = part
        for n in range(4):
            rs1s[k, n] = part[:, n * 256 : (n + 1) * 256].astype(BF16)
        for d in (1, 3, 2):
            na = lax.rem(a + d, 4)
            remote(rs1s.at[k, na], rs1r.at[k, a], r1_ss, r1_rs.at[k, a], a_dev(na)).start()

    def stage1(k):
        total = acc[k % 2, :, ds(a * 256, 256, 256)]
        for d in (1, 3, 2):
            na = lax.rem(a + d, 4)
            arrived(rs1r.at[k, na], r1_rs.at[k, na])
            total = total + rs1r[k, na].astype(F32)
        tot_v[k % 2] = total
        rs2s[k] = total.astype(BF16)
        for d in (1, 3, 2):
            nb = lax.rem(b + d, 4)
            remote(
                rs2s.at[k, ds(nb * 32, 32, 32)], rs2r.at[k, b], r2_ss, r2_rs.at[k, b], b_dev(nb)
            ).start()

    def block(k, na, nb=None, pc=c):
        row = pc * PIECE + k * FC
        rows = ds(row, FC, FC) if nb is None else ds(row + nb * 32, 32, 32)
        return wbuf.at[rows, ds(na * 256, 256, 256)]

    def stage2(k):
        total = tot_v[k % 2, ds(b * 32, 32, 32), :]
        for d in (1, 3, 2):
            nb = lax.rem(b + d, 4)
            arrived(rs2r.at[k, nb], r2_rs.at[k, nb])
            total = total + rs2r[k, nb].astype(F32)
        final = block(k, a, b)
        final[...] = total.astype(BF16)
        for d in (1, 3, 2):
            remote(final, final, ab_ss, ab_rs.at[k, b], b_dev(lax.rem(b + d, 4))).start()

    def stage3(k):
        for d in (1, 3, 2):
            nb = lax.rem(b + d, 4)
            arrived(block(k, a, nb), ab_rs.at[k, nb])
        whole = block(k, a)
        for d in (1, 3, 2):
            remote(whole, whole, aa_ss, aa_rs.at[k, a], a_dev(lax.rem(a + d, 4))).start()
        remote(whole, whole, ac_ss, ac_rs.at[k, a], partner).start()

    def stage4(k):
        for d in (1, 3, 2):
            na = lax.rem(a + d, 4)
            whole = block(k, na)
            arrived(whole, aa_rs.at[k, na])
            remote(whole, whole, ac_ss, ac_rs.at[k, na], partner).start()

    def stage5(k):
        for n in range(4):
            arrived(block(k, n, pc=1 - c), ac_rs.at[k, n])

    stages = (stage0, stage1, stage2, stage3, stage4, stage5)
    for t in range(NC + len(stages) - 1):
        for i, stage in enumerate(stages):
            if 0 <= t - i < NC:
                stage(t - i)
        send_more(2)
        if t == 0:
            for dz, dc in ZPEERS:
                src = lax.rem(g + dz, 4) * 2 + lax.rem(c + dc, 2)
                arrived(gbuf1.at[src], g1_rs.at[src])
            total = gbuf1[0]
            for i in range(1, 8):
                total = total + gbuf1[i]
            gbuf2[x] = total
            g_copies += broadcast(
                gbuf2, x, [plane(lax.rem(x + d, 4), y, c) for d in (1, 3, 2)], g2_ss, g2_rs
            )
        if t == 3:
            for d in (1, 3, 2):
                px = lax.rem(x + d, 4)
                arrived(gbuf2.at[px], g2_rs.at[px])
            gbuf3[y] = (gbuf2[0] + gbuf2[1]) + (gbuf2[2] + gbuf2[3])
            g_copies += broadcast(
                gbuf3, y, [plane(x, lax.rem(y + d, 4), c) for d in (1, 3, 2)], g3_ss, g3_rs
            )
    out = pltpu.make_async_copy(wbuf, w_out, in_sem.at[0])
    out.start()

    for d in (1, 3, 2):
        py = lax.rem(y + d, 4)
        arrived(gbuf3.at[py], g3_rs.at[py])
    total = (gbuf3[0] + gbuf3[1]) + (gbuf3[2] + gbuf3[3])
    g_out[...] = total[:, :D]
    kg_out[...] = total[:, D:]

    def sent(ref, ss):
        remote(ref, ref, ss, ss, (g, l)).wait_send()

    for copy in g_copies:
        copy.wait_send()
    sent(hbuf.at[:, ds(0, 7 * ROWS)], h_ss)
    sent(gkbuf.at[ds(0, 4 * ROWS)], k_ss)
    sent(gkbuf.at[ds(0, 3 * ROWS)], rel_ss)
    sent(rs1s.at[:, ds(0, 3)], r1_ss)
    sent(rs2s.at[:, ds(0, 96)], r2_ss)
    sent(rs2s.at[:, ds(0, 96)], ab_ss)
    sent(rs1s.at[:, ds(0, 3)], aa_ss)
    sent(rs1s, ac_ss)
    own.wait()
    everyone = remote(slots_v.at[ds(0, 31 * PAIR)], slots_out.at[ds(0, 31 * PAIR)], s_ss, s_rs, (g, l))
    everyone.wait_send()
    everyone.wait_recv()
    out.wait()


def body(hidden, cotangent, importance, block_len, version, destination, w_key, in_gain, key_gain):
    dma = pltpu.SemaphoreType.DMA
    vmem = pl.BlockSpec(memory_space=pltpu.VMEM)
    hbm = pl.BlockSpec(memory_space=pl.ANY)
    slots, w_rows, gain_grad, kgain_grad = pl.pallas_call(
        kernel,
        name="grad_step",
        out_shape=(
            jax.ShapeDtypeStruct((SR, D), BF16),
            jax.ShapeDtypeStruct((D // 4, KD), BF16),
            jax.ShapeDtypeStruct((1, D), F32),
            jax.ShapeDtypeStruct((1, HD), F32),
        ),
        in_specs=[hbm, hbm, vmem, vmem, vmem, vmem, hbm, vmem, vmem],
        out_specs=(hbm, hbm, vmem, vmem),
        scratch_shapes=[
            pltpu.VMEM((ROWS, D), BF16),
            pltpu.VMEM((D, KD), BF16),
            pltpu.VMEM((ROWS, KD), BF16),
            pltpu.VMEM((ROWS, HD), F32),
            pltpu.VMEM((ROWS, HD), F32),
            pltpu.VMEM((ROWS, D), BF16),
            pltpu.VMEM((ROWS, HD), F32),
            pltpu.VMEM((SR, ROWS), BF16),
            pltpu.VMEM((SR, D), BF16),
            pltpu.VMEM((NC, 8 * ROWS, FC), BF16),
            pltpu.VMEM((8 * ROWS, KD), BF16),
            pltpu.VMEM((2, FC, KD), F32),
            pltpu.VMEM((2, FC, 256), F32),
            pltpu.VMEM((NC, 4, FC, 256), BF16),
            pltpu.VMEM((NC, 4, FC, 256), BF16),
            pltpu.VMEM((NC, FC, 256), BF16),
            pltpu.VMEM((NC, 4, 32, 256), BF16),
            pltpu.VMEM((D // 4, KD), BF16),
            pltpu.VMEM((8, 1, D + HD), F32),
            pltpu.VMEM((4, 1, D + HD), F32),
            pltpu.VMEM((4, 1, D + HD), F32),
            dma((5,)), dma((4,)), dma(()),
            dma(()), dma((NC, 8)), dma(()), dma((8,)), dma(()), dma(()), dma(()),
            dma(()), dma((NC, 4)), dma(()), dma((NC, 4)),
            dma(()), dma((NC, 4)), dma(()), dma((NC, 4)), dma(()), dma((NC, 4)),
            dma((7,)), dma((8,)), dma((3,)), dma((4,)), dma((3,)), dma((4,)),
        ],
        compiler_params=pltpu.CompilerParams(
            collective_id=0, has_side_effects=True, vmem_limit_bytes=50 * 1024 * 1024
        ),
    )(
        hidden, cotangent, importance.reshape(1, ROWS), block_len.reshape(1, 32),
        version.reshape(1, 32), destination.reshape(1, 32), w_key, in_gain.reshape(1, D), key_gain.reshape(1, HD),
    )
    return slots, w_rows.astype(F32), gain_grad[0], kgain_grad[0]


def solution(mesh):
    return jax.shard_map(
        body,
        mesh=mesh,
        in_specs=(
            P(("gen", "learn"), None),
            P(("gen", "learn"), None),
            P(("gen", "learn")),
            P(("gen", "learn")),
            P(("gen", "learn")),
            P(("gen", "learn"), None),
            P(),
            P(),
            P(),
        ),
        out_specs=(P(("gen", "learn"), None), P("gen", None), P(), P()),
        check_vma=False,
    )
```

```python
import functools

import jax
import jax.numpy as jnp
from jax import lax
from jax.experimental import pallas as pl
from jax.experimental.pallas import tpu as pltpu
from jax.sharding import PartitionSpec as P

MESH = pl.DeviceIdType.MESH
F32 = jnp.float32
BF16 = jnp.bfloat16

D = 5120
KD = 1024
HD = 128
ROWS = 256
TILE = 8
SR = 512
PAIR = 16
PIECE = D // 8
FC = 128
NC = PIECE // FC
TW = 256
EPS = 1e-06

OTHERS = (
    (1, 0), (3, 0), (0, 1), (0, 3), (1, 1), (3, 3), (1, 3), (3, 1),
    (2, 0), (0, 2), (2, 1), (1, 2), (2, 3), (3, 2), (2, 2),
)
ORDER = ((0, 0, 1),) + tuple((a, b, c) for (a, b) in OTHERS for c in range(2))
ZPEERS = ((0, 1), (1, 0), (3, 0), (1, 1), (3, 1), (2, 0), (2, 1))


SLOT_GROUPS = (3, 2, 1, 1, 2, 2, 2, 1, 1, 1, 0)


def ds(start, size, mult=None):
    return pl.ds(start if mult is None else pl.multiple_of(start, mult), size)


def kernel(
    hid, cot, imp, blen, ver, dest, w, gain, kgain,
    slots_out, wbuf, g_out,
    x_v, w_v, cot_v, inv_v, cw_v, h_v, msum_v, place_v, slots_v, hbuf, gkbuf, acc, tot_v,
    rs1s, rs1r, rs2s, rs2r, gbuf1, gbuf2, gbuf3,
    in_sem, w_sem, own_sem, h_ss, h_rs, k_ss, k_rs, rel_ss, s_ss, s_rs,
    r1_ss, r1_rs, r2_ss, r2_rs, ab_ss, ab_rs, aa_ss, aa_rs, ac_ss, ac_rs,
    g1_ss, g1_rs, g2_ss, g2_rs, g3_ss, g3_rs,
):
    g = lax.axis_index("gen")
    l = lax.axis_index("learn")
    x = l // 8
    y = (l // 2) % 4
    c = l % 2
    a = x + c * (y - x)
    b = y + c * (x - y)
    me = g * 2 + c

    def plane(px, py, pc):
        return (g, px * 8 + py * 2 + pc)

    def a_dev(na):
        return plane(x + (1 - c) * (na - x), y + c * (na - y), c)

    def b_dev(nb):
        return plane(x + c * (nb - x), y + (1 - c) * (nb - y), c)

    def z_dev(q, pc):
        return (q, x * 8 + y * 2 + pc)

    def remote(src, dst, ss, rs, dev):
        return pltpu.make_async_remote_copy(src, dst, ss, rs, device_id=dev, device_id_type=MESH)

    for i in range(4):
        rows = ds(i * 64, 64)
        pltpu.make_async_copy(hid.at[rows], x_v.at[rows], in_sem.at[i]).start()
    for n in range(4):
        cols = ds(n * 256, 256)
        pltpu.make_async_copy(w.at[:, cols], w_v.at[:, cols], w_sem.at[n]).start()
    pltpu.make_async_copy(cot, cot_v, in_sem.at[4]).start()

    barrier = pltpu.get_barrier_semaphore()

    @pl.loop(1, 32)
    def _(i):
        pl.semaphore_signal(barrier, inc=1, device_id=(g, lax.rem(l + i, 32)), device_id_type=MESH)

    for dz, dc in ZPEERS[1:]:
        pl.semaphore_signal(
            barrier, inc=1, device_id=z_dev(lax.rem(g + dz, 4), lax.rem(c + dc, 2)), device_id_type=MESH
        )

    r256 = lax.broadcasted_iota(jnp.int32, (ROWS, ROWS), 0)
    j256 = lax.broadcasted_iota(jnp.int32, (ROWS, ROWS), 1)
    imp_col = jnp.sum(jnp.where(r256 == j256, imp[...], 0.0), axis=1, keepdims=True)
    r32 = lax.broadcasted_iota(jnp.int32, (ROWS, 32), 0)
    j32 = lax.broadcasted_iota(jnp.int32, (ROWS, 32), 1)
    of_block = (r32 >> 3) == j32
    len_col = jnp.sum(jnp.where(of_block, blen[...].astype(F32), 0.0), axis=1, keepdims=True)
    ver_col = jnp.sum(jnp.where(of_block, ver[...].astype(F32), 0.0), axis=1, keepdims=True)
    row_col = (lax.broadcasted_iota(jnp.int32, (ROWS, 1), 0) & 7).astype(F32)
    inside = jnp.where(row_col < len_col, 1.0, 0.0)
    age = 3.0 - ver_col
    decay = jnp.where(age == 0.0, 1.0, jnp.where(age == 1.0, 0.5, jnp.where(age == 2.0, 0.25, 0.125)))
    cw_v[...] = jnp.broadcast_to(jnp.minimum(imp_col, 2.0) * (decay * inside), (ROWS, HD))

    @pl.loop(0, 4)
    def _(i):
        big = ds(i * 64, 64, 64)
        pltpu.make_async_copy(hid.at[big], x_v.at[big], in_sem.at[i]).wait()
        invs = []
        for k in range(4):
            rows = ds(i * 64 + k * 16, 16, 16)
            total = jnp.zeros((16, HD), F32)
            for f in range(D // HD):
                xf = x_v[rows, f * HD : (f + 1) * HD].astype(F32)
                total = total + xf * xf
            inv = lax.rsqrt(jnp.sum(total, axis=1, keepdims=True) * (1.0 / D) + EPS)
            inv = jnp.broadcast_to(inv, (16, HD))
            inv_v[rows, :] = inv
            invs.append(inv)
        for k in range(4):
            rows = ds(i * 64 + k * 16, 16, 16)
            for f in range(D // HD):
                cols = slice(f * HD, (f + 1) * HD)
                h_v[rows, cols] = (x_v[rows, cols].astype(F32) * invs[k] * gain[:, cols]).astype(BF16)

    def mine(ref):
        return ref.at[ds(me * ROWS, ROWS, ROWS)]

    def send_h(k):
        for dz, dc in ZPEERS:
            q, pc = lax.rem(g + dz, 4), lax.rem(c + dc, 2)
            piece = h_v.at[:, ds((q * 2 + pc) * PIECE + k * FC, FC, FC)]
            remote(piece, mine(hbuf.at[k]), h_ss, h_rs.at[k, me], z_dev(q, pc)).start()

    def place_rows():
        b32 = lax.broadcasted_iota(jnp.int32, (32, 32), 0)
        e32 = lax.broadcasted_iota(jnp.int32, (32, 32), 1)
        dest_col = jnp.sum(jnp.where(b32 == e32, dest[...].astype(F32), 0.0), axis=1, keepdims=True)
        blk = lax.broadcasted_iota(jnp.int32, (32, ROWS), 0)
        row_blk = lax.broadcasted_iota(jnp.int32, (32, ROWS), 1) >> 3
        dest_row = jnp.sum(jnp.where(blk == row_blk, dest_col, 0.0), axis=0, keepdims=True)
        rank_row = jnp.sum(jnp.where((blk < row_blk) & (dest_col == dest_row), 1.0, 0.0), axis=0, keepdims=True)
        target = dest_row * 2.0 + rank_row
        srow = lax.broadcasted_iota(jnp.int32, (SR, ROWS), 0)
        scol = lax.broadcasted_iota(jnp.int32, (SR, ROWS), 1)
        hit = ((srow >> 3).astype(F32) == target) & ((srow & 7) == (scol & 7))
        place_v[...] = jnp.where(hit, 1.0, 0.0).astype(BF16)

    pltpu.make_async_copy(cot, cot_v, in_sem.at[4]).wait()
    for n in range(4):
        cols = ds(n * 256, 256)
        pltpu.make_async_copy(w.at[:, cols], w_v.at[:, cols], w_sem.at[n]).wait()
    kg = jnp.zeros((1, HD), F32)
    for n in range(4):
        keys = jnp.dot(h_v[...], w_v[:, n * 256 : (n + 1) * 256], preferred_element_type=F32)
        for s in range(2):
            k = keys[:, s * HD : (s + 1) * HD]
            head = slice(n * 256 + s * HD, n * 256 + s * HD + HD)
            scale = lax.rsqrt(jnp.sum(k * k, axis=1, keepdims=True) * (1.0 / HD) + EPS)
            up = (cot_v[:, head].astype(F32) * cw_v[...]).astype(BF16).astype(F32)
            kg = kg + jnp.sum(up * k * scale, axis=0, keepdims=True)
            u = up * kgain[...]
            mean = jnp.sum(u * k, axis=1, keepdims=True) * (1.0 / HD)
            gk = (scale * u - k * (scale * scale * scale) * mean).astype(BF16)
            gkbuf[ds(me * ROWS, ROWS, ROWS), head] = gk
            if n + s == 0:
                msum_v[...] = gk.astype(F32) * k
            else:
                msum_v[...] += gk.astype(F32) * k
        if n == 0:
            pl.semaphore_wait(barrier, 31 + 6)
            send_h(0)
            place_rows()
    gbuf1[me, :, D:] = kg

    for dz, dc in ((1, 0), (3, 0), (0, 1)):
        q, pc = lax.rem(g + dz, 4), lax.rem(c + dc, 2)
        remote(mine(gkbuf), mine(gkbuf), k_ss, k_rs.at[me], z_dev(q, pc)).start()
    send_h(1)
    for k in range(NC):
        hbuf[k, ds(me * ROWS, ROWS, ROWS), :] = h_v[:, ds(me * PIECE + k * FC, FC, FC)]

    mean = jnp.sum(msum_v[...], axis=1, keepdims=True) * (1.0 / D)
    msum_v[...] = jnp.broadcast_to(mean, (ROWS, HD))

    def send_slots(q, order):
        quarter = ds(q * 1280, 1280, 1280)
        for dx, dy, dc in order:
            dev = plane(lax.rem(x + dx, 4), lax.rem(y + dy, 4), lax.rem(c + dc, 2))
            remote(
                slots_v.at[ds(dev[1] * PAIR, PAIR, PAIR), quarter],
                slots_out.at[ds(l * PAIR, PAIR, PAIR), quarter],
                s_ss, s_rs, dev,
            ).start()

    def quarter_of(q):
        for s in range(1280 // TW):
            cols = pl.ds(pl.multiple_of(q * 1280 + s * TW, TW), TW)
            grad_h = lax.dot_general(
                mine(gkbuf)[...], w_v[cols, :], (((1,), (1,)), ((), ())), preferred_element_type=F32
            )
            inv = jnp.concatenate([inv_v[...]] * (TW // HD), axis=1)
            mean = jnp.concatenate([msum_v[...]] * (TW // HD), axis=1)
            normed = x_v[:, cols].astype(F32) * inv
            gbuf1[me, :, cols] = jnp.sum(grad_h * normed, axis=0, keepdims=True)
            grad_in = (inv * (grad_h * gain[:, cols] - normed * mean)).astype(BF16)
            slots_v[:, cols] = jnp.dot(place_v[...], grad_in, preferred_element_type=F32).astype(BF16)

    @pl.loop(0, 2)
    def _(q):
        quarter_of(q)
        send_slots(q, ORDER)

    @pl.loop(2, 4)
    def _(q):
        quarter_of(q)

    own_rows = ds(l * PAIR, PAIR, PAIR)
    own = pltpu.make_async_copy(slots_v.at[own_rows], slots_out.at[own_rows], own_sem)
    own.start()
    groups = [ORDER[i : i + 4] for i in range(0, 31, 4)]
    held_back = [(q, order) for q in (2, 3) for order in groups]

    def send_more(count):
        for _ in range(count):
            if held_back:
                send_slots(*held_back.pop(0))

    def broadcast(buf, place, peers, ss, rs):
        copies = []
        for i, dev in enumerate(peers):
            copy = remote(buf.at[place], buf.at[place], ss.at[i], rs.at[place], dev)
            copy.start()
            copies.append(copy)
        return copies

    def arrived(ref, rs):
        remote(ref, ref, rs, rs, (g, l)).wait_recv()

    g_copies = broadcast(
        gbuf1, me, [z_dev(lax.rem(g + dz, 4), lax.rem(c + dc, 2)) for dz, dc in ZPEERS], g1_ss, g1_rs
    )
    partner = z_dev(g, 1 - c)

    def of(ref, src):
        return ref.at[ds(src * ROWS, ROWS, ROWS)]

    def hand_on(src, rows, dev):
        ref = gkbuf.at[rows]
        remote(ref, ref, rel_ss, k_rs.at[src], dev).start()

    for step in (1, 3):
        src = lax.rem(g + step, 4) * 2 + c
        arrived(of(gkbuf, src), k_rs.at[src])
        half = ds(src * ROWS + (step // 2) * (ROWS // 2), ROWS // 2, ROWS // 2)
        hand_on(src, half, z_dev(lax.rem(g + 4 - step, 4), c))
    for k in range(2, NC):
        send_h(k)
    for step in (1, 3, 2):
        src = lax.rem(g + step, 4) * 2 + c
        if step == 2:
            arrived(of(gkbuf, src), k_rs.at[src])
        hand_on(src, ds(src * ROWS, ROWS, ROWS), partner)
    for dz in (0, 1, 3, 2):
        cross = lax.rem(g + dz, 4) * 2 + 1 - c
        arrived(of(gkbuf, cross), k_rs.at[cross])

    def stage0(k):
        for dz, dc in ZPEERS:
            src = lax.rem(g + dz, 4) * 2 + lax.rem(c + dc, 2)
            arrived(of(hbuf.at[k], src), h_rs.at[k, src])
        part = lax.dot_general(
            hbuf[k], gkbuf[...], (((0,), (0,)), ((), ())), preferred_element_type=F32
        )
        acc[k % 3] = part
        for n in range(4):
            rs1s[k, n] = part[:, n * 256 : (n + 1) * 256].astype(BF16)
        for d in (1, 3, 2):
            na = lax.rem(a + d, 4)
            remote(rs1s.at[k, na], rs1r.at[k, a], r1_ss, r1_rs.at[k, a], a_dev(na)).start()

    def stage1(k):
        total = acc[k % 3, :, ds(a * 256, 256, 256)]
        for d in (1, 3, 2):
            na = lax.rem(a + d, 4)
            arrived(rs1r.at[k, na], r1_rs.at[k, na])
            total = total + rs1r[k, na].astype(F32)
        tot_v[k % 2] = total
        rs2s[k] = total.astype(BF16)
        for d in (1, 3, 2):
            nb = lax.rem(b + d, 4)
            remote(
                rs2s.at[k, ds(nb * 32, 32, 32)], rs2r.at[k, b], r2_ss, r2_rs.at[k, b], b_dev(nb)
            ).start()

    def block(k, na, nb=None, pc=c):
        row = pc * PIECE + k * FC
        rows = ds(row, FC, FC) if nb is None else ds(row + nb * 32, 32, 32)
        return wbuf.at[rows, ds(na * 256, 256, 256)]

    def stage2(k):
        total = tot_v[k % 2, ds(b * 32, 32, 32), :]
        for d in (1, 3, 2):
            nb = lax.rem(b + d, 4)
            arrived(rs2r.at[k, nb], r2_rs.at[k, nb])
            total = total + rs2r[k, nb].astype(F32)
        final = block(k, a, b)
        final[...] = total.astype(BF16)
        for d in (1, 3, 2):
            remote(final, final, ab_ss, ab_rs.at[k, b], b_dev(lax.rem(b + d, 4))).start()

    def stage3(k):
        for d in (1, 3, 2):
            nb = lax.rem(b + d, 4)
            arrived(block(k, a, nb), ab_rs.at[k, nb])
        whole = block(k, a)
        for d in (1, 3, 2):
            remote(whole, whole, aa_ss, aa_rs.at[k, a], a_dev(lax.rem(a + d, 4))).start()
        remote(whole, whole, ac_ss, ac_rs.at[k, a], partner).start()

    def stage4(k):
        for d in (1, 3, 2):
            na = lax.rem(a + d, 4)
            whole = block(k, na)
            arrived(whole, aa_rs.at[k, na])
            remote(whole, whole, ac_ss, ac_rs.at[k, na], partner).start()

    def stage5(k):
        for n in range(4):
            arrived(block(k, n, pc=1 - c), ac_rs.at[k, n])

    stages = (stage0, stage1, stage2, stage3, stage4, stage5)
    lags = (0, 2, 3, 4, 5, 6)
    for t in range(NC + lags[-1]):
        for stage, lag in zip(stages, lags):
            if 0 <= t - lag < NC:
                stage(t - lag)
            if lag == 0:
                send_more(SLOT_GROUPS[t])
        if t == 5:
            for dz, dc in ZPEERS:
                src = lax.rem(g + dz, 4) * 2 + lax.rem(c + dc, 2)
                arrived(gbuf1.at[src], g1_rs.at[src])
            total = gbuf1[0]
            for i in range(1, 8):
                total = total + gbuf1[i]
            gbuf2[x] = total
            g_copies += broadcast(
                gbuf2, x, [plane(lax.rem(x + d, 4), y, c) for d in (1, 3, 2)], g2_ss, g2_rs
            )
        if t == 7:
            for d in (1, 3, 2):
                px = lax.rem(x + d, 4)
                arrived(gbuf2.at[px], g2_rs.at[px])
            gbuf3[y] = (gbuf2[0] + gbuf2[1]) + (gbuf2[2] + gbuf2[3])
            g_copies += broadcast(
                gbuf3, y, [plane(x, lax.rem(y + d, 4), c) for d in (1, 3, 2)], g3_ss, g3_rs
            )
    for d in (1, 3, 2):
        py = lax.rem(y + d, 4)
        arrived(gbuf3.at[py], g3_rs.at[py])
    total = (gbuf3[0] + gbuf3[1]) + (gbuf3[2] + gbuf3[3])
    g_out[...] = total

    def sent(ref, ss):
        remote(ref, ref, ss, ss, (g, l)).wait_send()

    for copy in g_copies:
        copy.wait_send()
    sent(hbuf.at[:, ds(0, 7 * ROWS)], h_ss)
    sent(gkbuf.at[ds(0, 3 * ROWS)], k_ss)
    sent(gkbuf.at[ds(0, 4 * ROWS)], rel_ss)
    sent(rs1s.at[:, ds(0, 3)], r1_ss)
    sent(rs2s.at[:, ds(0, 96)], r2_ss)
    sent(rs2s.at[:, ds(0, 96)], ab_ss)
    sent(rs1s.at[:, ds(0, 3)], aa_ss)
    sent(rs1s, ac_ss)
    own.wait()
    everyone = remote(slots_v.at[ds(0, 31 * PAIR)], slots_out.at[ds(0, 31 * PAIR)], s_ss, s_rs, (g, l))
    everyone.wait_send()
    everyone.wait_recv()


def finish(slots, w_rows, gains, slots_out, w_out, gain_out, kgain_out, f_v, sem):
    copies = [
        pltpu.make_async_copy(gains.at[:, ds(0, D)], gain_out, sem.at[0]),
        pltpu.make_async_copy(gains.at[:, ds(D, HD)], kgain_out, sem.at[1]),
        pltpu.make_async_copy(slots, slots_out, sem.at[2]),
    ]
    for copy in copies:
        copy.start()
    for i in range(4):
        rows = slice(i * 320, (i + 1) * 320)
        f_v[rows, :] = w_rows[rows, :].astype(F32)
        copy = pltpu.make_async_copy(f_v.at[ds(i * 320, 320)], w_out.at[ds(i * 320, 320)], sem.at[3 + i])
        copy.start()
        copies.append(copy)
    for copy in copies:
        copy.wait()


def body(hidden, cotangent, importance, block_len, version, destination, w_key, in_gain, key_gain):
    dma = pltpu.SemaphoreType.DMA
    vmem = pl.BlockSpec(memory_space=pltpu.VMEM)
    hbm = pl.BlockSpec(memory_space=pl.ANY)
    slots, w_rows, gains = pl.pallas_call(
        kernel,
        name="grad_step",
        out_shape=(
            pltpu.VMEM((SR, D), BF16),
            pltpu.VMEM((D // 4, KD), BF16),
            pltpu.VMEM((1, D + HD), F32),
        ),
        in_specs=[hbm, hbm, vmem, vmem, vmem, vmem, hbm, vmem, vmem],
        out_specs=(vmem, vmem, vmem),
        scratch_shapes=[
            pltpu.VMEM((ROWS, D), BF16),
            pltpu.VMEM((D, KD), BF16),
            pltpu.VMEM((ROWS, KD), BF16),
            pltpu.VMEM((ROWS, HD), F32),
            pltpu.VMEM((ROWS, HD), F32),
            pltpu.VMEM((ROWS, D), BF16),
            pltpu.VMEM((ROWS, HD), F32),
            pltpu.VMEM((SR, ROWS), BF16),
            pltpu.VMEM((SR, D), BF16),
            pltpu.VMEM((NC, 8 * ROWS, FC), BF16),
            pltpu.VMEM((8 * ROWS, KD), BF16),
            pltpu.VMEM((3, FC, KD), F32),
            pltpu.VMEM((2, FC, 256), F32),
            pltpu.VMEM((NC, 4, FC, 256), BF16),
            pltpu.VMEM((NC, 4, FC, 256), BF16),
            pltpu.VMEM((NC, FC, 256), BF16),
            pltpu.VMEM((NC, 4, 32, 256), BF16),
            pltpu.VMEM((8, 1, D + HD), F32),
            pltpu.VMEM((4, 1, D + HD), F32),
            pltpu.VMEM((4, 1, D + HD), F32),
            dma((5,)), dma((4,)), dma(()),
            dma(()), dma((NC, 8)), dma(()), dma((8,)), dma(()), dma(()), dma(()),
            dma(()), dma((NC, 4)), dma(()), dma((NC, 4)),
            dma(()), dma((NC, 4)), dma(()), dma((NC, 4)), dma(()), dma((NC, 4)),
            dma((7,)), dma((8,)), dma((3,)), dma((4,)), dma((3,)), dma((4,)),
        ],
        compiler_params=pltpu.CompilerParams(
            collective_id=0, has_side_effects=True, vmem_limit_bytes=50 * 1024 * 1024
        ),
    )(
        hidden, cotangent, importance.reshape(1, ROWS), block_len.reshape(1, 32),
        version.reshape(1, 32), destination.reshape(1, 32), w_key, in_gain.reshape(1, D), key_gain.reshape(1, HD),
    )
    slots, w_grad, gain_grad, kgain_grad = pl.pallas_call(
        finish,
        name="finish",
        out_shape=(
            jax.ShapeDtypeStruct((SR, D), BF16),
            jax.ShapeDtypeStruct((D // 4, KD), F32),
            jax.ShapeDtypeStruct((1, D), F32),
            jax.ShapeDtypeStruct((1, HD), F32),
        ),
        in_specs=[vmem, vmem, vmem],
        out_specs=(hbm, hbm, hbm, hbm),
        scratch_shapes=[
            pltpu.VMEM((D // 4, KD), F32),
            dma((7,)),
        ],
        compiler_params=pltpu.CompilerParams(vmem_limit_bytes=16 * 1024 * 1024),
    )(slots, w_rows, gains)
    return slots, w_grad, gain_grad[0], kgain_grad[0]


def solution(mesh):
    return jax.shard_map(
        body,
        mesh=mesh,
        in_specs=(
            P(("gen", "learn"), None),
            P(("gen", "learn"), None),
            P(("gen", "learn")),
            P(("gen", "learn")),
            P(("gen", "learn")),
            P(("gen", "learn"), None),
            P(),
            P(),
            P(),
        ),
        out_specs=(P(("gen", "learn"), None), P("gen", None), P(), P()),
        check_vma=False,
    )
```

```python
import functools

import jax
import jax.numpy as jnp
from jax import lax
from jax.experimental import pallas as pl
from jax.experimental.pallas import tpu as pltpu
from jax.sharding import PartitionSpec as P

MESH = pl.DeviceIdType.MESH
F32 = jnp.float32
BF16 = jnp.bfloat16

D = 5120
KD = 1024
HD = 128
ROWS = 256
TILE = 8
SR = 512
PAIR = 16
PIECE = D // 8
FC = 128
NC = PIECE // FC
TW = 256
EPS = 1e-06

OTHERS = (
    (1, 0), (3, 0), (0, 1), (0, 3), (1, 1), (3, 3), (1, 3), (3, 1),
    (2, 0), (0, 2), (2, 1), (1, 2), (2, 3), (3, 2), (2, 2),
)
EARLY = ((2, 2, 0), (2, 2, 1), (2, 0, 0), (0, 2, 0))
ORDER = ((0, 0, 1),) + tuple(
    (a, b, c) for (a, b) in OTHERS for c in range(2) if (a, b, c) not in EARLY
)
ZPEERS = ((0, 1), (1, 0), (3, 0), (1, 1), (3, 1), (2, 0), (2, 1))


MORE, GAINS = -1, -2
PLAN = (
    (0, 0), (MORE, 3), (0, 1), (MORE, 2), (0, 2), (MORE, 1), (1, 0), (0, 3), (MORE, 1), (1, 1), (2, 0),
    (0, 4), (MORE, 2), (1, 2), (1, 3), (MORE, 2), (1, 4), (GAINS, 0), (2, 1), (2, 2), (MORE, 2),
    (2, 3), (2, 4), (MORE, 2), (3, 0), (3, 1), (3, 2), (3, 3), (3, 4), (GAINS, 1), (MORE, 1),
    (4, 0), (4, 1), (4, 2), (4, 3), (4, 4), (5, 0), (5, 1), (5, 2), (5, 3), (5, 4),
)


def ds(start, size, mult=None):
    return pl.ds(start if mult is None else pl.multiple_of(start, mult), size)


def kernel(
    hid, cot, imp_h, blen_h, ver_h, dest_h, w, gain_h, kgain_h,
    slots_out, wbuf, g_out,
    x_v, w_v, cot_v, inv_v, cw_v, h_v, msum_v, place_v, slots_v, hbuf, gkbuf, acc, tot_v,
    rs1s, rs1r, rs2s, rs2r, gbuf1, gbuf2, gbuf3,
    imp, blen, ver, dest, gain, kgain,
    early_place, early_xs, early_ks, early_x, early_k, early_inv, early_sum, early_g,
    ex_ss, ex_rs, ek_ss, ek_rs,
    in_sem, w_sem, own_sem, h_ss, h_rs, k_ss, k_rs, rel_ss, s_ss, s_rs,
    r1_ss, r1_rs, r2_ss, r2_rs, ab_ss, ab_rs, aa_ss, aa_rs, ac_ss, ac_rs,
    g1_ss, g1_rs, g2_ss, g2_rs, g3_ss, g3_rs,
):
    g = lax.axis_index("gen")
    l = lax.axis_index("learn")
    x = l // 8
    y = (l // 2) % 4
    c = l % 2
    a = x + c * (y - x)
    b = y + c * (x - y)
    me = g * 2 + c

    def plane(px, py, pc):
        return (g, px * 8 + py * 2 + pc)

    def a_dev(na):
        return plane(x + (1 - c) * (na - x), y + c * (na - y), c)

    def b_dev(nb):
        return plane(x + c * (nb - x), y + (1 - c) * (nb - y), c)

    def z_dev(q, pc):
        return (q, x * 8 + y * 2 + pc)

    def remote(src, dst, ss, rs, dev):
        return pltpu.make_async_remote_copy(src, dst, ss, rs, device_id=dev, device_id_type=MESH)

    small = [
        pltpu.make_async_copy(src, dst, in_sem.at[5 + i])
        for i, (src, dst) in enumerate(
            ((gain_h, gain), (imp_h, imp), (blen_h, blen), (ver_h, ver), (dest_h, dest), (kgain_h, kgain))
        )
    ]
    for copy in small:
        copy.start()
    for i in range(4):
        rows = ds(i * 64, 64)
        pltpu.make_async_copy(hid.at[rows], x_v.at[rows], in_sem.at[i]).start()

    def load_w(n):
        cols = ds(n * 256, 256)
        return pltpu.make_async_copy(w.at[:, cols], w_v.at[:, cols], w_sem.at[n])

    load_w(0).start()

    barrier = pltpu.get_barrier_semaphore()

    @pl.loop(1, 32)
    def _(i):
        pl.semaphore_signal(barrier, inc=1, device_id=(g, lax.rem(l + i, 32)), device_id_type=MESH)

    for dz, dc in ZPEERS[1:]:
        pl.semaphore_signal(
            barrier, inc=1, device_id=z_dev(lax.rem(g + dz, 4), lax.rem(c + dc, 2)), device_id_type=MESH
        )

    for copy in small:
        copy.wait()

    r256 = lax.broadcasted_iota(jnp.int32, (ROWS, ROWS), 0)
    j256 = lax.broadcasted_iota(jnp.int32, (ROWS, ROWS), 1)
    imp_col = jnp.sum(jnp.where(r256 == j256, imp[...], 0.0), axis=1, keepdims=True)
    r32 = lax.broadcasted_iota(jnp.int32, (ROWS, 32), 0)
    j32 = lax.broadcasted_iota(jnp.int32, (ROWS, 32), 1)
    of_block = (r32 >> 3) == j32
    len_col = jnp.sum(jnp.where(of_block, blen[...].astype(F32), 0.0), axis=1, keepdims=True)
    ver_col = jnp.sum(jnp.where(of_block, ver[...].astype(F32), 0.0), axis=1, keepdims=True)
    row_col = (lax.broadcasted_iota(jnp.int32, (ROWS, 1), 0) & 7).astype(F32)
    inside = jnp.where(row_col < len_col, 1.0, 0.0)
    age = 3.0 - ver_col
    decay = jnp.where(age == 0.0, 1.0, jnp.where(age == 1.0, 0.5, jnp.where(age == 2.0, 0.25, 0.125)))
    cw_v[...] = jnp.broadcast_to(jnp.minimum(imp_col, 2.0) * (decay * inside), (ROWS, HD))

    b32 = lax.broadcasted_iota(jnp.int32, (32, 32), 0)
    e32 = lax.broadcasted_iota(jnp.int32, (32, 32), 1)
    dest_col = jnp.sum(jnp.where(b32 == e32, dest[...].astype(F32), 0.0), axis=1, keepdims=True)
    blk = lax.broadcasted_iota(jnp.int32, (32, ROWS), 0)
    row_blk = lax.broadcasted_iota(jnp.int32, (32, ROWS), 1) >> 3
    dest_row = jnp.sum(jnp.where(blk == row_blk, dest_col, 0.0), axis=0, keepdims=True)
    rank_row = jnp.sum(jnp.where((blk < row_blk) & (dest_col == dest_row), 1.0, 0.0), axis=0, keepdims=True)
    target = dest_row * 2.0 + rank_row
    srow = lax.broadcasted_iota(jnp.int32, (SR, ROWS), 0)
    scol = lax.broadcasted_iota(jnp.int32, (SR, ROWS), 1)
    hit = ((srow >> 3).astype(F32) == target) & ((srow & 7) == (scol & 7))
    place_v[...] = jnp.where(hit, 1.0, 0.0).astype(BF16)

    @pl.loop(0, 4)
    def _(i):
        big = ds(i * 64, 64, 64)
        pltpu.make_async_copy(hid.at[big], x_v.at[big], in_sem.at[i]).wait()
        invs = []
        for k in range(4):
            rows = ds(i * 64 + k * 16, 16, 16)
            total = jnp.zeros((16, HD), F32)
            for f in range(D // HD):
                xf = x_v[rows, f * HD : (f + 1) * HD].astype(F32)
                total = total + xf * xf
            inv = lax.rsqrt(jnp.sum(total, axis=1, keepdims=True) * (1.0 / D) + EPS)
            inv = jnp.broadcast_to(inv, (16, HD))
            inv_v[rows, :] = inv
            invs.append(inv)
        for k in range(4):
            rows = ds(i * 64 + k * 16, 16, 16)
            for f in range(D // HD):
                cols = slice(f * HD, (f + 1) * HD)
                h_v[rows, cols] = (x_v[rows, cols].astype(F32) * invs[k] * gain[:, cols]).astype(BF16)

    load_w(1).start()
    pltpu.make_async_copy(cot, cot_v, in_sem.at[4]).start()

    def mine(ref):
        return ref.at[ds(me * ROWS, ROWS, ROWS)]

    def send_h(k):
        for dz, dc in ZPEERS:
            q, pc = lax.rem(g + dz, 4), lax.rem(c + dc, 2)
            piece = h_v.at[:, ds((q * 2 + pc) * PIECE + k * FC, FC, FC)]
            remote(piece, mine(hbuf.at[k]), h_ss, h_rs.at[k, me], z_dev(q, pc)).start()

    early = [
        plane(lax.rem(x + dx, 4), lax.rem(y + dy, 4), lax.rem(c + dc, 2)) for dx, dy, dc in EARLY
    ]

    def of_early(e):
        return ds(e * PAIR, PAIR)

    def send_early(src, dst, ss, rs):
        for e, dev in enumerate(early):
            remote(src.at[of_early(e)], dst.at[of_early(e)], ss, rs.at[e], dev).start()

    for e, dev in enumerate(early):
        early_place[of_early(e), :] = place_v[ds(dev[1] * PAIR, PAIR, PAIR), :]
    for f in range(0, D, TW):
        early_xs[:, f : f + TW] = jnp.dot(
            early_place[...], x_v[:, f : f + TW], preferred_element_type=F32
        ).astype(BF16)

    load_w(2).start()
    load_w(3).start()
    pl.semaphore_wait(barrier, 31 + 6)
    send_early(early_xs, early_x, ex_ss, ex_rs)
    send_h(0)

    pltpu.make_async_copy(cot, cot_v, in_sem.at[4]).wait()
    kg = jnp.zeros((1, HD), F32)
    for n in range(4):
        load_w(n).wait()
        keys = jnp.dot(h_v[...], w_v[:, n * 256 : (n + 1) * 256], preferred_element_type=F32)
        for s in range(2):
            k = keys[:, s * HD : (s + 1) * HD]
            head = slice(n * 256 + s * HD, n * 256 + s * HD + HD)
            scale = lax.rsqrt(jnp.sum(k * k, axis=1, keepdims=True) * (1.0 / HD) + EPS)
            up = (cot_v[:, head].astype(F32) * cw_v[...]).astype(BF16).astype(F32)
            kg = kg + jnp.sum(up * k * scale, axis=0, keepdims=True)
            u = up * kgain[...]
            mean = jnp.sum(u * k, axis=1, keepdims=True) * (1.0 / HD)
            gk = (scale * u - k * (scale * scale * scale) * mean).astype(BF16)
            gkbuf[ds(me * ROWS, ROWS, ROWS), head] = gk
            if n + s == 0:
                msum_v[...] = gk.astype(F32) * k
            else:
                msum_v[...] += gk.astype(F32) * k
    gbuf1[me, :, D:] = kg

    for dz, dc in ((1, 0), (3, 0), (0, 1)):
        q, pc = lax.rem(g + dz, 4), lax.rem(c + dc, 2)
        remote(mine(gkbuf), mine(gkbuf), k_ss, k_rs.at[me], z_dev(q, pc)).start()
    early_ks[...] = jnp.dot(early_place[...], mine(gkbuf)[...], preferred_element_type=F32).astype(BF16)
    send_early(early_ks, early_k, ek_ss, ek_rs)
    send_h(1)
    for k in range(NC):
        hbuf[k, ds(me * ROWS, ROWS, ROWS), :] = h_v[:, ds(me * PIECE + k * FC, FC, FC)]

    mean = jnp.sum(msum_v[...], axis=1, keepdims=True) * (1.0 / D)
    msum_v[...] = jnp.broadcast_to(mean, (ROWS, HD))

    def send_slots(q, order):
        quarter = ds(q * 1280, 1280, 1280)
        for dx, dy, dc in order:
            dev = plane(lax.rem(x + dx, 4), lax.rem(y + dy, 4), lax.rem(c + dc, 2))
            remote(
                slots_v.at[ds(dev[1] * PAIR, PAIR, PAIR), quarter],
                slots_out.at[ds(l * PAIR, PAIR, PAIR), quarter],
                s_ss, s_rs, dev,
            ).start()

    def quarter_of(q):
        for s in range(1280 // TW):
            cols = pl.ds(pl.multiple_of(q * 1280 + s * TW, TW), TW)
            grad_h = lax.dot_general(
                mine(gkbuf)[...], w_v[cols, :], (((1,), (1,)), ((), ())), preferred_element_type=F32
            )
            inv = jnp.concatenate([inv_v[...]] * (TW // HD), axis=1)
            mean = jnp.concatenate([msum_v[...]] * (TW // HD), axis=1)
            normed = x_v[:, cols].astype(F32) * inv
            gbuf1[me, :, cols] = jnp.sum(grad_h * normed, axis=0, keepdims=True)
            grad_in = (inv * (grad_h * gain[:, cols] - normed * mean)).astype(BF16)
            slots_v[:, cols] = jnp.dot(place_v[...], grad_in, preferred_element_type=F32).astype(BF16)

    @pl.loop(0, 2)
    def _(q):
        quarter_of(q)
        send_slots(q, ORDER)

    @pl.loop(2, 4)
    def _(q):
        quarter_of(q)

    own_rows = ds(l * PAIR, PAIR, PAIR)
    own = pltpu.make_async_copy(slots_v.at[own_rows], slots_out.at[own_rows], own_sem)
    own.start()
    groups = [ORDER[i : i + 4] for i in range(0, len(ORDER), 4)]
    held_back = [(q, order) for q in (2, 3) for order in groups]

    def send_more(count):
        for _ in range(count):
            if held_back:
                send_slots(*held_back.pop(0))

    def broadcast(buf, place, peers, ss, rs):
        copies = []
        for i, dev in enumerate(peers):
            copy = remote(buf.at[place], buf.at[place], ss.at[i], rs.at[place], dev)
            copy.start()
            copies.append(copy)
        return copies

    def arrived(ref, rs):
        remote(ref, ref, rs, rs, (g, l)).wait_recv()

    g_copies = broadcast(
        gbuf1, me, [z_dev(lax.rem(g + dz, 4), lax.rem(c + dc, 2)) for dz, dc in ZPEERS], g1_ss, g1_rs
    )
    partner = z_dev(g, 1 - c)

    def of(ref, src):
        return ref.at[ds(src * ROWS, ROWS, ROWS)]

    def hand_on(src, rows, dev):
        ref = gkbuf.at[rows]
        remote(ref, ref, rel_ss, k_rs.at[src], dev).start()

    for step in (1, 3):
        src = lax.rem(g + step, 4) * 2 + c
        arrived(of(gkbuf, src), k_rs.at[src])
        half = ds(src * ROWS + (step // 2) * (ROWS // 2), ROWS // 2, ROWS // 2)
        hand_on(src, half, z_dev(lax.rem(g + 4 - step, 4), c))
    for k in range(2, NC):
        send_h(k)
    for step in (1, 3):
        src = lax.rem(g + step, 4) * 2 + c
        hand_on(src, ds(src * ROWS, ROWS, ROWS), partner)

    for e in range(len(EARLY)):
        arrived(early_x.at[of_early(e)], ex_rs.at[e])
        arrived(early_k.at[of_early(e)], ek_rs.at[e])
    invs = []
    for e in range(len(EARLY)):
        total = jnp.zeros((PAIR, HD), F32)
        for f in range(0, D, HD):
            xf = early_x[of_early(e), f : f + HD].astype(F32)
            total = total + xf * xf
        invs.append(lax.rsqrt(jnp.sum(total, axis=1, keepdims=True) * (1.0 / D) + EPS))
    early_inv[...] = jnp.broadcast_to(jnp.concatenate(invs, axis=0), (len(EARLY) * PAIR, HD))
    early_sum[...] = jnp.zeros_like(early_sum)

    @pl.loop(0, D // 1024)
    def _(i):
        inv = jnp.concatenate([early_inv[...]] * 2, axis=1)
        for s in range(4):
            cols = pl.ds(pl.multiple_of(i * 1024 + s * TW, TW), TW)
            grad_h = lax.dot_general(
                early_k[...], w_v[cols, :], (((1,), (1,)), ((), ())), preferred_element_type=F32
            )
            grad = grad_h * gain[:, cols]
            early_g[:, cols] = grad
            prod = grad * (early_x[:, cols].astype(F32) * inv)
            early_sum[...] += prod[:, :HD] + prod[:, HD:]

    mean = jnp.sum(early_sum[...], axis=1, keepdims=True) * (1.0 / D)
    early_sum[...] = jnp.broadcast_to(mean, early_sum.shape)

    @pl.loop(0, D // 1280)
    def _(i):
        for e, dev in enumerate(early):
            for s in range(1280 // HD):
                cols = pl.ds(pl.multiple_of(i * 1280 + s * HD, HD), HD)
                rows = of_early(e)
                inv = early_inv[rows, :]
                normed = early_x[rows, cols].astype(F32) * inv
                grad_in = inv * (early_g[rows, cols] - normed * early_sum[rows, :])
                slots_out[ds(dev[1] * PAIR, PAIR, PAIR), cols] = grad_in.astype(BF16)

    for step in (2,):
        src = lax.rem(g + step, 4) * 2 + c
        if step == 2:
            arrived(of(gkbuf, src), k_rs.at[src])
        hand_on(src, ds(src * ROWS, ROWS, ROWS), partner)
    for dz in (0, 1, 3, 2):
        cross = lax.rem(g + dz, 4) * 2 + 1 - c
        arrived(of(gkbuf, cross), k_rs.at[cross])

    def stage0(k):
        for dz, dc in ZPEERS:
            src = lax.rem(g + dz, 4) * 2 + lax.rem(c + dc, 2)
            arrived(of(hbuf.at[k], src), h_rs.at[k, src])
        part = lax.dot_general(
            hbuf[k], gkbuf[...], (((0,), (0,)), ((), ())), preferred_element_type=F32
        )
        acc[k % 4] = part
        for n in range(4):
            rs1s[k, n] = part[:, n * 256 : (n + 1) * 256].astype(BF16)
        for d in (1, 3, 2):
            na = lax.rem(a + d, 4)
            remote(rs1s.at[k, na], rs1r.at[k, a], r1_ss, r1_rs.at[k, a], a_dev(na)).start()

    def stage1(k):
        total = acc[k % 4, :, ds(a * 256, 256, 256)]
        for d in (1, 3, 2):
            na = lax.rem(a + d, 4)
            arrived(rs1r.at[k, na], r1_rs.at[k, na])
            total = total + rs1r[k, na].astype(F32)
        tot_v[k] = total
        rs2s[k] = total.astype(BF16)
        for d in (1, 3, 2):
            nb = lax.rem(b + d, 4)
            remote(
                rs2s.at[k, ds(nb * 32, 32, 32)], rs2r.at[k, b], r2_ss, r2_rs.at[k, b], b_dev(nb)
            ).start()

    def block(k, na, nb=None, pc=c):
        row = pc * PIECE + k * FC
        rows = ds(row, FC, FC) if nb is None else ds(row + nb * 32, 32, 32)
        return wbuf.at[rows, ds(na * 256, 256, 256)]

    def stage2(k):
        total = tot_v[k, ds(b * 32, 32, 32), :]
        for d in (1, 3, 2):
            nb = lax.rem(b + d, 4)
            arrived(rs2r.at[k, nb], r2_rs.at[k, nb])
            total = total + rs2r[k, nb].astype(F32)
        final = block(k, a, b)
        final[...] = total.astype(BF16)
        for d in (1, 3, 2):
            remote(final, final, ab_ss, ab_rs.at[k, b], b_dev(lax.rem(b + d, 4))).start()

    def stage3(k):
        for d in (1, 3, 2):
            nb = lax.rem(b + d, 4)
            arrived(block(k, a, nb), ab_rs.at[k, nb])
        whole = block(k, a)
        for d in (1, 3, 2):
            remote(whole, whole, aa_ss, aa_rs.at[k, a], a_dev(lax.rem(a + d, 4))).start()
        remote(whole, whole, ac_ss, ac_rs.at[k, a], partner).start()

    def stage4(k):
        for d in (1, 3, 2):
            na = lax.rem(a + d, 4)
            whole = block(k, na)
            arrived(whole, aa_rs.at[k, na])
            remote(whole, whole, ac_ss, ac_rs.at[k, na], partner).start()

    def stage5(k):
        for n in range(4):
            arrived(block(k, n, pc=1 - c), ac_rs.at[k, n])

    def gains_over_x():
        for dz, dc in ZPEERS:
            src = lax.rem(g + dz, 4) * 2 + lax.rem(c + dc, 2)
            arrived(gbuf1.at[src], g1_rs.at[src])
        total = gbuf1[0]
        for i in range(1, 8):
            total = total + gbuf1[i]
        gbuf2[x] = total
        return broadcast(gbuf2, x, [plane(lax.rem(x + d, 4), y, c) for d in (1, 3, 2)], g2_ss, g2_rs)

    def gains_over_y():
        for d in (1, 3, 2):
            px = lax.rem(x + d, 4)
            arrived(gbuf2.at[px], g2_rs.at[px])
        gbuf3[y] = (gbuf2[0] + gbuf2[1]) + (gbuf2[2] + gbuf2[3])
        return broadcast(gbuf3, y, [plane(x, lax.rem(y + d, 4), c) for d in (1, 3, 2)], g3_ss, g3_rs)

    stages = (stage0, stage1, stage2, stage3, stage4, stage5)
    for what, n in PLAN:
        if what == MORE:
            send_more(n)
        elif what == GAINS:
            g_copies += (gains_over_x, gains_over_y)[n]()
        else:
            stages[what](n)

    for d in (1, 3, 2):
        py = lax.rem(y + d, 4)
        arrived(gbuf3.at[py], g3_rs.at[py])
    total = (gbuf3[0] + gbuf3[1]) + (gbuf3[2] + gbuf3[3])
    g_out[...] = total

    def sent(ref, ss):
        remote(ref, ref, ss, ss, (g, l)).wait_send()

    for copy in g_copies:
        copy.wait_send()
    sent(hbuf.at[:, ds(0, 7 * ROWS)], h_ss)
    sent(gkbuf.at[ds(0, 3 * ROWS)], k_ss)
    sent(gkbuf.at[ds(0, 4 * ROWS)], rel_ss)
    sent(rs1s.at[:, ds(0, 3)], r1_ss)
    sent(rs2s.at[:, ds(0, 96)], r2_ss)
    sent(rs2s.at[:, ds(0, 96)], ab_ss)
    sent(rs1s.at[:, ds(0, 3)], aa_ss)
    sent(rs1s, ac_ss)
    own.wait()
    sent(early_xs, ex_ss)
    sent(early_ks, ek_ss)
    rest = ds(0, len(ORDER) * PAIR)
    everyone = remote(slots_v.at[rest], slots_out.at[rest], s_ss, s_rs, (g, l))
    everyone.wait_send()
    everyone.wait_recv()


def finish(slots, w_rows, gains, slots_out, w_out, gain_out, kgain_out, f_v, sem):
    copies = [
        pltpu.make_async_copy(gains.at[:, ds(0, D)], gain_out, sem.at[0]),
        pltpu.make_async_copy(gains.at[:, ds(D, HD)], kgain_out, sem.at[1]),
        pltpu.make_async_copy(slots, slots_out, sem.at[2]),
    ]
    for copy in copies:
        copy.start()
    for i in range(4):
        rows = slice(i * 320, (i + 1) * 320)
        f_v[rows, :] = w_rows[rows, :].astype(F32)
        copy = pltpu.make_async_copy(f_v.at[ds(i * 320, 320)], w_out.at[ds(i * 320, 320)], sem.at[3 + i])
        copy.start()
        copies.append(copy)
    for copy in copies:
        copy.wait()


def body(hidden, cotangent, importance, block_len, version, destination, w_key, in_gain, key_gain):
    dma = pltpu.SemaphoreType.DMA
    vmem = pl.BlockSpec(memory_space=pltpu.VMEM)
    hbm = pl.BlockSpec(memory_space=pl.ANY)
    slots, w_rows, gains = pl.pallas_call(
        kernel,
        name="grad_step",
        out_shape=(
            pltpu.VMEM((SR, D), BF16),
            pltpu.VMEM((D // 4, KD), BF16),
            pltpu.VMEM((1, D + HD), F32),
        ),
        in_specs=[hbm] * 9,
        out_specs=(vmem, vmem, vmem),
        scratch_shapes=[
            pltpu.VMEM((ROWS, D), BF16),
            pltpu.VMEM((D, KD), BF16),
            pltpu.VMEM((ROWS, KD), BF16),
            pltpu.VMEM((ROWS, HD), F32),
            pltpu.VMEM((ROWS, HD), F32),
            pltpu.VMEM((ROWS, D), BF16),
            pltpu.VMEM((ROWS, HD), F32),
            pltpu.VMEM((SR, ROWS), BF16),
            pltpu.VMEM((SR, D), BF16),
            pltpu.VMEM((NC, 8 * ROWS, FC), BF16),
            pltpu.VMEM((8 * ROWS, KD), BF16),
            pltpu.VMEM((4, FC, KD), F32),
            pltpu.VMEM((NC, FC, 256), F32),
            pltpu.VMEM((NC, 4, FC, 256), BF16),
            pltpu.VMEM((NC, 4, FC, 256), BF16),
            pltpu.VMEM((NC, FC, 256), BF16),
            pltpu.VMEM((NC, 4, 32, 256), BF16),
            pltpu.VMEM((8, 1, D + HD), F32),
            pltpu.VMEM((4, 1, D + HD), F32),
            pltpu.VMEM((4, 1, D + HD), F32),
            pltpu.VMEM((1, ROWS), F32),
            pltpu.VMEM((1, 32), jnp.int32),
            pltpu.VMEM((1, 32), jnp.int32),
            pltpu.VMEM((1, 32), jnp.int32),
            pltpu.VMEM((1, D), F32),
            pltpu.VMEM((1, HD), F32),
            pltpu.VMEM((len(EARLY) * PAIR, ROWS), BF16),
            pltpu.VMEM((len(EARLY) * PAIR, D), BF16),
            pltpu.VMEM((len(EARLY) * PAIR, KD), BF16),
            pltpu.VMEM((len(EARLY) * PAIR, D), BF16),
            pltpu.VMEM((len(EARLY) * PAIR, KD), BF16),
            pltpu.VMEM((len(EARLY) * PAIR, HD), F32),
            pltpu.VMEM((len(EARLY) * PAIR, HD), F32),
            pltpu.VMEM((len(EARLY) * PAIR, D), F32),
            dma(()), dma((len(EARLY),)), dma(()), dma((len(EARLY),)),
            dma((11,)), dma((4,)), dma(()),
            dma(()), dma((NC, 8)), dma(()), dma((8,)), dma(()), dma(()), dma(()),
            dma(()), dma((NC, 4)), dma(()), dma((NC, 4)),
            dma(()), dma((NC, 4)), dma(()), dma((NC, 4)), dma(()), dma((NC, 4)),
            dma((7,)), dma((8,)), dma((3,)), dma((4,)), dma((3,)), dma((4,)),
        ],
        compiler_params=pltpu.CompilerParams(
            collective_id=0, has_side_effects=True, vmem_limit_bytes=50 * 1024 * 1024
        ),
    )(
        hidden, cotangent, importance.reshape(1, ROWS), block_len.reshape(1, 32),
        version.reshape(1, 32), destination.reshape(1, 32), w_key, in_gain.reshape(1, D), key_gain.reshape(1, HD),
    )
    slots, w_grad, gain_grad, kgain_grad = pl.pallas_call(
        finish,
        name="finish",
        out_shape=(
            jax.ShapeDtypeStruct((SR, D), BF16),
            jax.ShapeDtypeStruct((D // 4, KD), F32),
            jax.ShapeDtypeStruct((1, D), F32),
            jax.ShapeDtypeStruct((1, HD), F32),
        ),
        in_specs=[vmem, vmem, vmem],
        out_specs=(hbm, hbm, hbm, hbm),
        scratch_shapes=[
            pltpu.VMEM((D // 4, KD), F32),
            dma((7,)),
        ],
        compiler_params=pltpu.CompilerParams(vmem_limit_bytes=16 * 1024 * 1024),
    )(slots, w_rows, gains)
    return slots, w_grad, gain_grad[0], kgain_grad[0]


def solution(mesh):
    return jax.shard_map(
        body,
        mesh=mesh,
        in_specs=(
            P(("gen", "learn"), None),
            P(("gen", "learn"), None),
            P(("gen", "learn")),
            P(("gen", "learn")),
            P(("gen", "learn")),
            P(("gen", "learn"), None),
            P(),
            P(),
            P(),
        ),
        out_specs=(P(("gen", "learn"), None), P("gen", None), P(), P()),
        check_vma=False,
    )
```

```python
import functools

import jax
import jax.numpy as jnp
from jax import lax
from jax.experimental import pallas as pl
from jax.experimental.pallas import tpu as pltpu
from jax.sharding import PartitionSpec as P

MESH = pl.DeviceIdType.MESH
F32 = jnp.float32
BF16 = jnp.bfloat16

D = 5120
KD = 1024
HD = 128
ROWS = 256
TILE = 8
SR = 512
PAIR = 16
PIECE = D // 8
FC = 128
NC = PIECE // FC
TW = 256
EPS = 1e-06

OTHERS = (
    (1, 0), (3, 0), (0, 1), (0, 3), (1, 1), (3, 3), (1, 3), (3, 1),
    (2, 0), (0, 2), (2, 1), (1, 2), (2, 3), (3, 2), (2, 2),
)
EARLY = ((2, 2, 0), (2, 2, 1), (2, 0, 0), (0, 2, 0))
ORDER = ((0, 0, 1),) + tuple(
    (a, b, c) for c in range(2) for (a, b) in OTHERS if (a, b, c) not in EARLY
)
ZPEERS = ((0, 1), (1, 0), (3, 0), (1, 1), (3, 1), (2, 0), (2, 1))


MORE, GAINS = -1, -2
PLAN = (
    (0, 0), (MORE, 3), (0, 1), (MORE, 2), (0, 2), (MORE, 1), (1, 0), (0, 3), (MORE, 1), (1, 1),
    (2, 0), (0, 4), (MORE, 2), (1, 2), (2, 1), (3, 0), (1, 3), (MORE, 1), (1, 4), (GAINS, 0),
    (2, 2), (3, 1), (MORE, 1), (2, 3), (4, 0), (2, 4), (MORE, 2), (3, 2), (4, 1), (3, 3), (3, 4),
    (GAINS, 1), (MORE, 2), (4, 2), (4, 3), (4, 4), (MORE, 1), (5, 0), (5, 1), (5, 2), (5, 3),
    (5, 4),
)


def ds(start, size, mult=None):
    return pl.ds(start if mult is None else pl.multiple_of(start, mult), size)


def kernel(
    hid, cot, imp_h, blen_h, ver_h, dest_h, w, gain_h, kgain_h,
    slots_out, wbuf, g_out,
    x_v, w_v, cot_v, inv_v, cw_v, h_v, msum_v, place_v, slots_v, hbuf, gkbuf, acc, tot_v,
    rs1s, rs1r, rs2s, rs2r, gbuf1, gbuf2, gbuf3,
    imp, blen, ver, dest, gain, kgain,
    early_place, early_xs, early_ks, early_x, early_k, early_inv, early_sum, early_g,
    ex_ss, ex_rs, ek_ss, ek_rs,
    in_sem, w_sem, own_sem, h_ss, h_rs, k_ss, k_rs, rel_ss, s_ss, s_rs,
    r1_ss, r1_rs, r2_ss, r2_rs, ab_ss, ab_rs, aa_ss, aa_rs, ac_ss, ac_rs,
    g1_ss, g1_rs, g2_ss, g2_rs, g3_ss, g3_rs,
):
    g = lax.axis_index("gen")
    l = lax.axis_index("learn")
    x = l // 8
    y = (l // 2) % 4
    c = l % 2
    a = x + c * (y - x)
    b = y + c * (x - y)
    me = g * 2 + c

    def plane(px, py, pc):
        return (g, px * 8 + py * 2 + pc)

    def a_dev(na):
        return plane(x + (1 - c) * (na - x), y + c * (na - y), c)

    def b_dev(nb):
        return plane(x + c * (nb - x), y + (1 - c) * (nb - y), c)

    def z_dev(q, pc):
        return (q, x * 8 + y * 2 + pc)

    def remote(src, dst, ss, rs, dev):
        return pltpu.make_async_remote_copy(src, dst, ss, rs, device_id=dev, device_id_type=MESH)

    small = [
        pltpu.make_async_copy(src, dst, in_sem.at[5 + i])
        for i, (src, dst) in enumerate(
            ((gain_h, gain), (imp_h, imp), (blen_h, blen), (ver_h, ver), (dest_h, dest), (kgain_h, kgain))
        )
    ]
    for copy in small:
        copy.start()
    for i in range(4):
        rows = ds(i * 64, 64)
        pltpu.make_async_copy(hid.at[rows], x_v.at[rows], in_sem.at[i]).start()

    def load_w(n):
        cols = ds(n * 256, 256)
        return pltpu.make_async_copy(w.at[:, cols], w_v.at[:, cols], w_sem.at[n])

    load_w(0).start()

    barrier = pltpu.get_barrier_semaphore()

    @pl.loop(1, 32)
    def _(i):
        pl.semaphore_signal(barrier, inc=1, device_id=(g, lax.rem(l + i, 32)), device_id_type=MESH)

    for dz, dc in ZPEERS[1:]:
        pl.semaphore_signal(
            barrier, inc=1, device_id=z_dev(lax.rem(g + dz, 4), lax.rem(c + dc, 2)), device_id_type=MESH
        )

    for copy in small:
        copy.wait()

    r256 = lax.broadcasted_iota(jnp.int32, (ROWS, ROWS), 0)
    j256 = lax.broadcasted_iota(jnp.int32, (ROWS, ROWS), 1)
    imp_col = jnp.sum(jnp.where(r256 == j256, imp[...], 0.0), axis=1, keepdims=True)
    r32 = lax.broadcasted_iota(jnp.int32, (ROWS, 32), 0)
    j32 = lax.broadcasted_iota(jnp.int32, (ROWS, 32), 1)
    of_block = (r32 >> 3) == j32
    len_col = jnp.sum(jnp.where(of_block, blen[...].astype(F32), 0.0), axis=1, keepdims=True)
    ver_col = jnp.sum(jnp.where(of_block, ver[...].astype(F32), 0.0), axis=1, keepdims=True)
    row_col = (lax.broadcasted_iota(jnp.int32, (ROWS, 1), 0) & 7).astype(F32)
    inside = jnp.where(row_col < len_col, 1.0, 0.0)
    age = 3.0 - ver_col
    decay = jnp.where(age == 0.0, 1.0, jnp.where(age == 1.0, 0.5, jnp.where(age == 2.0, 0.25, 0.125)))
    cw_v[...] = jnp.broadcast_to(jnp.minimum(imp_col, 2.0) * (decay * inside), (ROWS, HD))

    b32 = lax.broadcasted_iota(jnp.int32, (32, 32), 0)
    e32 = lax.broadcasted_iota(jnp.int32, (32, 32), 1)
    dest_col = jnp.sum(jnp.where(b32 == e32, dest[...].astype(F32), 0.0), axis=1, keepdims=True)
    blk = lax.broadcasted_iota(jnp.int32, (32, ROWS), 0)
    row_blk = lax.broadcasted_iota(jnp.int32, (32, ROWS), 1) >> 3
    dest_row = jnp.sum(jnp.where(blk == row_blk, dest_col, 0.0), axis=0, keepdims=True)
    rank_row = jnp.sum(jnp.where((blk < row_blk) & (dest_col == dest_row), 1.0, 0.0), axis=0, keepdims=True)
    target = dest_row * 2.0 + rank_row
    srow = lax.broadcasted_iota(jnp.int32, (SR, ROWS), 0)
    scol = lax.broadcasted_iota(jnp.int32, (SR, ROWS), 1)
    hit = ((srow >> 3).astype(F32) == target) & ((srow & 7) == (scol & 7))
    place_v[...] = jnp.where(hit, 1.0, 0.0).astype(BF16)

    @pl.loop(0, 4)
    def _(i):
        big = ds(i * 64, 64, 64)
        pltpu.make_async_copy(hid.at[big], x_v.at[big], in_sem.at[i]).wait()
        invs = []
        for k in range(4):
            rows = ds(i * 64 + k * 16, 16, 16)
            total = jnp.zeros((16, HD), F32)
            for f in range(D // HD):
                xf = x_v[rows, f * HD : (f + 1) * HD].astype(F32)
                total = total + xf * xf
            inv = lax.rsqrt(jnp.sum(total, axis=1, keepdims=True) * (1.0 / D) + EPS)
            inv = jnp.broadcast_to(inv, (16, HD))
            inv_v[rows, :] = inv
            invs.append(inv)
        for k in range(4):
            rows = ds(i * 64 + k * 16, 16, 16)
            for f in range(D // HD):
                cols = slice(f * HD, (f + 1) * HD)
                h_v[rows, cols] = (x_v[rows, cols].astype(F32) * invs[k] * gain[:, cols]).astype(BF16)

    load_w(1).start()
    pltpu.make_async_copy(cot, cot_v, in_sem.at[4]).start()

    def mine(ref):
        return ref.at[ds(me * ROWS, ROWS, ROWS)]

    def send_h(k):
        for dz, dc in ZPEERS:
            q, pc = lax.rem(g + dz, 4), lax.rem(c + dc, 2)
            piece = h_v.at[:, ds((q * 2 + pc) * PIECE + k * FC, FC, FC)]
            remote(piece, mine(hbuf.at[k]), h_ss, h_rs.at[k, me], z_dev(q, pc)).start()

    early = [
        plane(lax.rem(x + dx, 4), lax.rem(y + dy, 4), lax.rem(c + dc, 2)) for dx, dy, dc in EARLY
    ]

    def of_early(e):
        return ds(e * PAIR, PAIR)

    def send_early(src, dst, ss, rs):
        for e, dev in enumerate(early):
            remote(src.at[of_early(e)], dst.at[of_early(e)], ss, rs.at[e], dev).start()

    for e, dev in enumerate(early):
        early_place[of_early(e), :] = place_v[ds(dev[1] * PAIR, PAIR, PAIR), :]
    for f in range(0, D, TW):
        early_xs[:, f : f + TW] = jnp.dot(
            early_place[...], x_v[:, f : f + TW], preferred_element_type=F32
        ).astype(BF16)

    load_w(2).start()
    load_w(3).start()
    pl.semaphore_wait(barrier, 31 + 6)
    send_early(early_xs, early_x, ex_ss, ex_rs)
    send_h(0)

    pltpu.make_async_copy(cot, cot_v, in_sem.at[4]).wait()
    kg = jnp.zeros((1, HD), F32)
    for n in range(4):
        load_w(n).wait()
        keys = jnp.dot(h_v[...], w_v[:, n * 256 : (n + 1) * 256], preferred_element_type=F32)
        for s in range(2):
            k = keys[:, s * HD : (s + 1) * HD]
            head = slice(n * 256 + s * HD, n * 256 + s * HD + HD)
            scale = lax.rsqrt(jnp.sum(k * k, axis=1, keepdims=True) * (1.0 / HD) + EPS)
            up = (cot_v[:, head].astype(F32) * cw_v[...]).astype(BF16).astype(F32)
            kg = kg + jnp.sum(up * k * scale, axis=0, keepdims=True)
            u = up * kgain[...]
            mean = jnp.sum(u * k, axis=1, keepdims=True) * (1.0 / HD)
            gk = (scale * u - k * (scale * scale * scale) * mean).astype(BF16)
            gkbuf[ds(me * ROWS, ROWS, ROWS), head] = gk
            if n + s == 0:
                msum_v[...] = gk.astype(F32) * k
            else:
                msum_v[...] += gk.astype(F32) * k
    gbuf1[me, :, D:] = kg

    for dz, dc in ((1, 0), (3, 0), (0, 1)):
        q, pc = lax.rem(g + dz, 4), lax.rem(c + dc, 2)
        remote(mine(gkbuf), mine(gkbuf), k_ss, k_rs.at[me], z_dev(q, pc)).start()
    early_ks[...] = jnp.dot(early_place[...], mine(gkbuf)[...], preferred_element_type=F32).astype(BF16)
    send_early(early_ks, early_k, ek_ss, ek_rs)
    send_h(1)
    for k in range(NC):
        hbuf[k, ds(me * ROWS, ROWS, ROWS), :] = h_v[:, ds(me * PIECE + k * FC, FC, FC)]

    mean = jnp.sum(msum_v[...], axis=1, keepdims=True) * (1.0 / D)
    msum_v[...] = jnp.broadcast_to(mean, (ROWS, HD))

    def send_slots(q, order):
        quarter = ds(q * 1280, 1280, 1280)
        for dx, dy, dc in order:
            dev = plane(lax.rem(x + dx, 4), lax.rem(y + dy, 4), lax.rem(c + dc, 2))
            remote(
                slots_v.at[ds(dev[1] * PAIR, PAIR, PAIR), quarter],
                slots_out.at[ds(l * PAIR, PAIR, PAIR), quarter],
                s_ss, s_rs, dev,
            ).start()

    def quarter_of(q):
        for s in range(1280 // TW):
            cols = pl.ds(pl.multiple_of(q * 1280 + s * TW, TW), TW)
            grad_h = lax.dot_general(
                mine(gkbuf)[...], w_v[cols, :], (((1,), (1,)), ((), ())), preferred_element_type=F32
            )
            inv = jnp.concatenate([inv_v[...]] * (TW // HD), axis=1)
            mean = jnp.concatenate([msum_v[...]] * (TW // HD), axis=1)
            normed = x_v[:, cols].astype(F32) * inv
            gbuf1[me, :, cols] = jnp.sum(grad_h * normed, axis=0, keepdims=True)
            grad_in = (inv * (grad_h * gain[:, cols] - normed * mean)).astype(BF16)
            slots_v[:, cols] = jnp.dot(place_v[...], grad_in, preferred_element_type=F32).astype(BF16)

    @pl.loop(0, 2)
    def _(q):
        quarter_of(q)
        send_slots(q, ORDER)

    @pl.loop(2, 4)
    def _(q):
        quarter_of(q)

    own_rows = ds(l * PAIR, PAIR, PAIR)
    own = pltpu.make_async_copy(slots_v.at[own_rows], slots_out.at[own_rows], own_sem)
    own.start()
    groups = [ORDER[i : i + 4] for i in range(0, len(ORDER), 4)]
    held_back = [(q, order) for q in (2, 3) for order in groups]

    def send_more(count):
        for _ in range(count):
            if held_back:
                send_slots(*held_back.pop(0))

    def broadcast(buf, place, peers, ss, rs):
        copies = []
        for i, dev in enumerate(peers):
            copy = remote(buf.at[place], buf.at[place], ss.at[i], rs.at[place], dev)
            copy.start()
            copies.append(copy)
        return copies

    def arrived(ref, rs):
        remote(ref, ref, rs, rs, (g, l)).wait_recv()

    g_copies = broadcast(
        gbuf1, me, [z_dev(lax.rem(g + dz, 4), lax.rem(c + dc, 2)) for dz, dc in ZPEERS], g1_ss, g1_rs
    )
    partner = z_dev(g, 1 - c)

    def of(ref, src):
        return ref.at[ds(src * ROWS, ROWS, ROWS)]

    def hand_on(src, rows, dev):
        ref = gkbuf.at[rows]
        remote(ref, ref, rel_ss, k_rs.at[src], dev).start()

    for step in (1, 3):
        src = lax.rem(g + step, 4) * 2 + c
        arrived(of(gkbuf, src), k_rs.at[src])
        half = ds(src * ROWS + (step // 2) * (ROWS // 2), ROWS // 2, ROWS // 2)
        hand_on(src, half, z_dev(lax.rem(g + 4 - step, 4), c))
    for k in range(2, NC):
        send_h(k)
    for step in (1, 3):
        src = lax.rem(g + step, 4) * 2 + c
        hand_on(src, ds(src * ROWS, ROWS, ROWS), partner)

    for e in range(len(EARLY)):
        arrived(early_x.at[of_early(e)], ex_rs.at[e])
        arrived(early_k.at[of_early(e)], ek_rs.at[e])
    invs = []
    for e in range(len(EARLY)):
        total = jnp.zeros((PAIR, HD), F32)
        for f in range(0, D, HD):
            xf = early_x[of_early(e), f : f + HD].astype(F32)
            total = total + xf * xf
        invs.append(lax.rsqrt(jnp.sum(total, axis=1, keepdims=True) * (1.0 / D) + EPS))
    early_inv[...] = jnp.broadcast_to(jnp.concatenate(invs, axis=0), (len(EARLY) * PAIR, HD))
    early_sum[...] = jnp.zeros_like(early_sum)

    @pl.loop(0, D // 1024)
    def _(i):
        inv = jnp.concatenate([early_inv[...]] * 2, axis=1)
        for s in range(4):
            cols = pl.ds(pl.multiple_of(i * 1024 + s * TW, TW), TW)
            grad_h = lax.dot_general(
                early_k[...], w_v[cols, :], (((1,), (1,)), ((), ())), preferred_element_type=F32
            )
            grad = grad_h * gain[:, cols]
            early_g[:, cols] = grad
            prod = grad * (early_x[:, cols].astype(F32) * inv)
            early_sum[...] += prod[:, :HD] + prod[:, HD:]

    mean = jnp.sum(early_sum[...], axis=1, keepdims=True) * (1.0 / D)
    early_sum[...] = jnp.broadcast_to(mean, early_sum.shape)

    @pl.loop(0, D // 1280)
    def _(i):
        for e, dev in enumerate(early):
            for s in range(1280 // HD):
                cols = pl.ds(pl.multiple_of(i * 1280 + s * HD, HD), HD)
                rows = of_early(e)
                inv = early_inv[rows, :]
                normed = early_x[rows, cols].astype(F32) * inv
                grad_in = inv * (early_g[rows, cols] - normed * early_sum[rows, :])
                slots_out[ds(dev[1] * PAIR, PAIR, PAIR), cols] = grad_in.astype(BF16)

    for step in (2,):
        src = lax.rem(g + step, 4) * 2 + c
        if step == 2:
            arrived(of(gkbuf, src), k_rs.at[src])
        hand_on(src, ds(src * ROWS, ROWS, ROWS), partner)
    for dz in (0, 1, 3, 2):
        cross = lax.rem(g + dz, 4) * 2 + 1 - c
        arrived(of(gkbuf, cross), k_rs.at[cross])

    def stage0(k):
        for dz, dc in ZPEERS:
            src = lax.rem(g + dz, 4) * 2 + lax.rem(c + dc, 2)
            arrived(of(hbuf.at[k], src), h_rs.at[k, src])
        part = lax.dot_general(
            hbuf[k], gkbuf[...], (((0,), (0,)), ((), ())), preferred_element_type=F32
        )
        acc[k % 4] = part
        for n in range(4):
            rs1s[k, n] = part[:, n * 256 : (n + 1) * 256].astype(BF16)
        for d in (1, 3, 2):
            na = lax.rem(a + d, 4)
            remote(rs1s.at[k, na], rs1r.at[k, a], r1_ss, r1_rs.at[k, a], a_dev(na)).start()

    def stage1(k):
        total = acc[k % 4, :, ds(a * 256, 256, 256)]
        for d in (1, 3, 2):
            na = lax.rem(a + d, 4)
            arrived(rs1r.at[k, na], r1_rs.at[k, na])
            total = total + rs1r[k, na].astype(F32)
        tot_v[k] = total
        rs2s[k] = total.astype(BF16)
        for d in (1, 3, 2):
            nb = lax.rem(b + d, 4)
            remote(
                rs2s.at[k, ds(nb * 32, 32, 32)], rs2r.at[k, b], r2_ss, r2_rs.at[k, b], b_dev(nb)
            ).start()

    def block(k, na, nb=None, pc=c):
        row = pc * PIECE + k * FC
        rows = ds(row, FC, FC) if nb is None else ds(row + nb * 32, 32, 32)
        return wbuf.at[rows, ds(na * 256, 256, 256)]

    def stage2(k):
        total = tot_v[k, ds(b * 32, 32, 32), :]
        for d in (1, 3, 2):
            nb = lax.rem(b + d, 4)
            arrived(rs2r.at[k, nb], r2_rs.at[k, nb])
            total = total + rs2r[k, nb].astype(F32)
        final = block(k, a, b)
        final[...] = total.astype(BF16)
        for d in (1, 3, 2):
            remote(final, final, ab_ss, ab_rs.at[k, b], b_dev(lax.rem(b + d, 4))).start()

    def stage3(k):
        for d in (1, 3, 2):
            nb = lax.rem(b + d, 4)
            arrived(block(k, a, nb), ab_rs.at[k, nb])
        whole = block(k, a)
        for d in (1, 3, 2):
            remote(whole, whole, aa_ss, aa_rs.at[k, a], a_dev(lax.rem(a + d, 4))).start()
        remote(whole, whole, ac_ss, ac_rs.at[k, a], partner).start()

    def stage4(k):
        for d in (1, 3, 2):
            na = lax.rem(a + d, 4)
            whole = block(k, na)
            arrived(whole, aa_rs.at[k, na])
            remote(whole, whole, ac_ss, ac_rs.at[k, na], partner).start()

    def stage5(k):
        for n in range(4):
            arrived(block(k, n, pc=1 - c), ac_rs.at[k, n])

    def gains_over_x():
        for dz, dc in ZPEERS:
            src = lax.rem(g + dz, 4) * 2 + lax.rem(c + dc, 2)
            arrived(gbuf1.at[src], g1_rs.at[src])
        total = gbuf1[0]
        for i in range(1, 8):
            total = total + gbuf1[i]
        gbuf2[x] = total
        return broadcast(gbuf2, x, [plane(lax.rem(x + d, 4), y, c) for d in (1, 3, 2)], g2_ss, g2_rs)

    def gains_over_y():
        for d in (1, 3, 2):
            px = lax.rem(x + d, 4)
            arrived(gbuf2.at[px], g2_rs.at[px])
        gbuf3[y] = (gbuf2[0] + gbuf2[1]) + (gbuf2[2] + gbuf2[3])
        return broadcast(gbuf3, y, [plane(x, lax.rem(y + d, 4), c) for d in (1, 3, 2)], g3_ss, g3_rs)

    stages = (stage0, stage1, stage2, stage3, stage4, stage5)
    for what, n in PLAN:
        if what == MORE:
            send_more(n)
        elif what == GAINS:
            g_copies += (gains_over_x, gains_over_y)[n]()
        else:
            stages[what](n)

    for d in (1, 3, 2):
        py = lax.rem(y + d, 4)
        arrived(gbuf3.at[py], g3_rs.at[py])
    total = (gbuf3[0] + gbuf3[1]) + (gbuf3[2] + gbuf3[3])
    g_out[...] = total

    def sent(ref, ss):
        remote(ref, ref, ss, ss, (g, l)).wait_send()

    for copy in g_copies:
        copy.wait_send()
    sent(hbuf.at[:, ds(0, 7 * ROWS)], h_ss)
    sent(gkbuf.at[ds(0, 3 * ROWS)], k_ss)
    sent(gkbuf.at[ds(0, 4 * ROWS)], rel_ss)
    sent(rs1s.at[:, ds(0, 3)], r1_ss)
    sent(rs2s.at[:, ds(0, 96)], r2_ss)
    sent(rs2s.at[:, ds(0, 96)], ab_ss)
    sent(rs1s.at[:, ds(0, 3)], aa_ss)
    sent(rs1s, ac_ss)
    own.wait()
    sent(early_xs, ex_ss)
    sent(early_ks, ek_ss)
    rest = ds(0, len(ORDER) * PAIR)
    everyone = remote(slots_v.at[rest], slots_out.at[rest], s_ss, s_rs, (g, l))
    everyone.wait_send()
    everyone.wait_recv()


def finish(slots, w_rows, gains, slots_out, w_out, gain_out, kgain_out, f_v, sem):
    copies = [
        pltpu.make_async_copy(gains.at[:, ds(0, D)], gain_out, sem.at[0]),
        pltpu.make_async_copy(gains.at[:, ds(D, HD)], kgain_out, sem.at[1]),
    ]
    for i in range(4):
        rows = ds(i * 128, 128)
        copies.append(pltpu.make_async_copy(slots.at[rows], slots_out.at[rows], sem.at[7 + i]))
    for copy in copies:
        copy.start()
    for i in range(4):
        rows = slice(i * 320, (i + 1) * 320)
        f_v[rows, :] = w_rows[rows, :].astype(F32)
        copy = pltpu.make_async_copy(f_v.at[ds(i * 320, 320)], w_out.at[ds(i * 320, 320)], sem.at[3 + i])
        copy.start()
        copies.append(copy)
    for copy in copies:
        copy.wait()


def body(hidden, cotangent, importance, block_len, version, destination, w_key, in_gain, key_gain):
    dma = pltpu.SemaphoreType.DMA
    vmem = pl.BlockSpec(memory_space=pltpu.VMEM)
    hbm = pl.BlockSpec(memory_space=pl.ANY)
    slots, w_rows, gains = pl.pallas_call(
        kernel,
        name="grad_step",
        out_shape=(
            pltpu.VMEM((SR, D), BF16),
            pltpu.VMEM((D // 4, KD), BF16),
            pltpu.VMEM((1, D + HD), F32),
        ),
        in_specs=[hbm] * 9,
        out_specs=(vmem, vmem, vmem),
        scratch_shapes=[
            pltpu.VMEM((ROWS, D), BF16),
            pltpu.VMEM((D, KD), BF16),
            pltpu.VMEM((ROWS, KD), BF16),
            pltpu.VMEM((ROWS, HD), F32),
            pltpu.VMEM((ROWS, HD), F32),
            pltpu.VMEM((ROWS, D), BF16),
            pltpu.VMEM((ROWS, HD), F32),
            pltpu.VMEM((SR, ROWS), BF16),
            pltpu.VMEM((SR, D), BF16),
            pltpu.VMEM((NC, 8 * ROWS, FC), BF16),
            pltpu.VMEM((8 * ROWS, KD), BF16),
            pltpu.VMEM((4, FC, KD), F32),
            pltpu.VMEM((NC, FC, 256), F32),
            pltpu.VMEM((NC, 4, FC, 256), BF16),
            pltpu.VMEM((NC, 4, FC, 256), BF16),
            pltpu.VMEM((NC, FC, 256), BF16),
            pltpu.VMEM((NC, 4, 32, 256), BF16),
            pltpu.VMEM((8, 1, D + HD), F32),
            pltpu.VMEM((4, 1, D + HD), F32),
            pltpu.VMEM((4, 1, D + HD), F32),
            pltpu.VMEM((1, ROWS), F32),
            pltpu.VMEM((1, 32), jnp.int32),
            pltpu.VMEM((1, 32), jnp.int32),
            pltpu.VMEM((1, 32), jnp.int32),
            pltpu.VMEM((1, D), F32),
            pltpu.VMEM((1, HD), F32),
            pltpu.VMEM((len(EARLY) * PAIR, ROWS), BF16),
            pltpu.VMEM((len(EARLY) * PAIR, D), BF16),
            pltpu.VMEM((len(EARLY) * PAIR, KD), BF16),
            pltpu.VMEM((len(EARLY) * PAIR, D), BF16),
            pltpu.VMEM((len(EARLY) * PAIR, KD), BF16),
            pltpu.VMEM((len(EARLY) * PAIR, HD), F32),
            pltpu.VMEM((len(EARLY) * PAIR, HD), F32),
            pltpu.VMEM((len(EARLY) * PAIR, D), F32),
            dma(()), dma((len(EARLY),)), dma(()), dma((len(EARLY),)),
            dma((11,)), dma((4,)), dma(()),
            dma(()), dma((NC, 8)), dma(()), dma((8,)), dma(()), dma(()), dma(()),
            dma(()), dma((NC, 4)), dma(()), dma((NC, 4)),
            dma(()), dma((NC, 4)), dma(()), dma((NC, 4)), dma(()), dma((NC, 4)),
            dma((7,)), dma((8,)), dma((3,)), dma((4,)), dma((3,)), dma((4,)),
        ],
        compiler_params=pltpu.CompilerParams(
            collective_id=0, has_side_effects=True, vmem_limit_bytes=50 * 1024 * 1024
        ),
    )(
        hidden, cotangent, importance.reshape(1, ROWS), block_len.reshape(1, 32),
        version.reshape(1, 32), destination.reshape(1, 32), w_key, in_gain.reshape(1, D), key_gain.reshape(1, HD),
    )
    slots, w_grad, gain_grad, kgain_grad = pl.pallas_call(
        finish,
        name="finish",
        out_shape=(
            jax.ShapeDtypeStruct((SR, D), BF16),
            jax.ShapeDtypeStruct((D // 4, KD), F32),
            jax.ShapeDtypeStruct((1, D), F32),
            jax.ShapeDtypeStruct((1, HD), F32),
        ),
        in_specs=[vmem, vmem, vmem],
        out_specs=(hbm, hbm, hbm, hbm),
        scratch_shapes=[
            pltpu.VMEM((D // 4, KD), F32),
            dma((11,)),
        ],
        compiler_params=pltpu.CompilerParams(vmem_limit_bytes=16 * 1024 * 1024),
    )(slots, w_rows, gains)
    return slots, w_grad, gain_grad[0], kgain_grad[0]


def solution(mesh):
    return jax.shard_map(
        body,
        mesh=mesh,
        in_specs=(
            P(("gen", "learn"), None),
            P(("gen", "learn"), None),
            P(("gen", "learn")),
            P(("gen", "learn")),
            P(("gen", "learn")),
            P(("gen", "learn"), None),
            P(),
            P(),
            P(),
        ),
        out_specs=(P(("gen", "learn"), None), P("gen", None), P(), P()),
        check_vma=False,
    )
```
